32 devices in a mesh: frame: 8 (over z, x), rec: 4 (over y, core).
Axes of the slice: x: 2, y: 2, z: 4, core: 2. Of those that a mesh axis runs over, the one named last changes fastest.
Arguments:
- inputs: bfloat16 [4, 8192, 512], P('rec', 'frame'), may hold values from -6 to 6
- conv_weight: bfloat16 [5, 512, 512], replicated, may hold values from -4 to 4
- conv_bias: float32 [512], replicated, may hold values from -3 to 3
- labels: int32 [4, 8192, 512], P('rec', 'frame'), may hold values 0 or 1
- rec_span: int32 [2, 4, 8192], P(None, 'rec', 'frame'), may hold values from 0 to 1023, as said below
Outputs:
- features: bfloat16 [4, 8192, 512], P('rec', 'frame')
- probe_weights: float32 [512, 512], replicated
The draws below stay inside these ranges and needn't reach their ends.
Inputs may be any that keep to these rules, and one draw needn't show every extreme that they name: Each stream is a series of whole recordings of at most 1024 frames, the last one possibly cut by the stream's end: rec_span[0, g, t] counts the frames of t's recording before t and rec_span[1, g, t] those after t within the stream; in every stream some recording has exactly 1024 frames.
All inputs are finite; a program needn't handle non-finite values. No bound on the sum of `labels` on one device may be relied on, other than what follows from the above.
Results may differ from the reference program's by a relative error of at most 0.0035.
The reference program's roundings to bfloat16 on the way (of `joined`) count: a program that leaves them out, or rounds other values in their place, can miss the bound.
Values may be sent and summed in bfloat16 or wider, within the bound.
A program may use at most 64 MiB of HBM per device.

```python
import math
import jax
import jax.numpy as jnp
from jax import lax

CIN = 512
FEAT = 512
LABELS = 512
TAPS = 5
REC_MOST = 1024
REC_MIN = 64
TIME = 8192
GROUPS = 4
FRAMES = 32768


def draw_rec_span(key, part):
    record_count = TIME // REC_MIN + 1
    stream_keys = jax.random.split(key, GROUPS)

    def one_stream(stream_key):
        length_key, pick_key = jax.random.split(stream_key)
        lengths = jax.random.randint(length_key, (record_count,), REC_MIN, REC_MOST + 1).astype(jnp.int32)
        longest = jax.random.randint(pick_key, (), 0, max(TIME // REC_MOST - 1, 1)).astype(jnp.int32)
        lengths = jnp.where(jnp.arange(record_count, dtype=jnp.int32) == longest, REC_MOST, lengths).astype(jnp.int32)
        record_ends = jnp.cumsum(lengths).astype(jnp.int32)
        record_starts = record_ends - lengths
        position = jnp.arange(TIME, dtype=jnp.int32)
        record_index = jnp.searchsorted(record_ends, position, side='right').astype(jnp.int32)
        before = position - record_starts[record_index]
        frames_after = jnp.minimum(record_ends[record_index], TIME) - 1 - position
        return jnp.stack([before, frames_after]).astype(jnp.int32)
    stream_spans = jax.vmap(one_stream)(stream_keys)
    return jnp.transpose(stream_spans, (1, 0, 2)).astype(jnp.int32)


def draw_conv_weight(key, part):
    base_key = jax.random.fold_in(key, 11)
    delta_key = jax.random.fold_in(key, 12)
    spread_key = jax.random.fold_in(key, 13)
    order_key = jax.random.fold_in(key, 14)
    family_count = FEAT // 4
    base = jnp.clip(jax.random.normal(base_key, (TAPS, CIN, family_count), jnp.float32), -3.0, 3.0)
    delta = jnp.clip(jax.random.normal(delta_key, (TAPS, CIN, FEAT), jnp.float32), -3.0, 3.0)
    spread = jnp.exp(jax.random.uniform(spread_key, (FEAT,), jnp.float32, math.log(0.02), 0.0))
    family = (jax.random.permutation(order_key, FEAT).astype(jnp.int32) // 4).astype(jnp.int32)
    picked = jnp.take(base, family, axis=2)
    weight = 6.0 / math.sqrt(TAPS * CIN) * (picked + spread[None, None, :] * delta)
    return weight.astype(jnp.float32).astype(jnp.bfloat16)


def plant(drawn, key, smallest, top_value):
    longest = drawn.shape.index(max(drawn.shape))
    spots = []
    for shift in (0, 1):
        where = [jax.random.randint(jax.random.fold_in(key, axis), (), 0, length) for axis, length in enumerate(drawn.shape)]
        where[longest] = (where[longest] + shift) % drawn.shape[longest]
        spots.append(tuple(where))
    return drawn.at[spots[0]].set(smallest).at[spots[1]].set(top_value)


def block_levels(rng, shape, cuts, low, high):
    def one(dim, blocks):
        draws = jax.random.uniform(jax.random.fold_in(jax.random.fold_in(rng, 6), dim), (blocks,), jnp.float32, low / len(cuts), high / len(cuts))
        return jnp.repeat(jnp.exp(draws), shape[dim] // blocks).reshape((-1,) + (1,) * (len(shape) - dim - 1))

    level = one(*cuts[0])
    for cut in cuts[1:]:
        level = level * one(*cut)
    return level


def noise(rng, extent, deviation, reach, cuts=(), kind=jnp.bfloat16):
    array = deviation * jax.random.normal(rng, extent, jnp.float32)
    if cuts:
        array = array * block_levels(rng, extent, cuts, -0.22, 0.18)
    return jnp.clip(array, -reach, reach).astype(kind)


def setup_inputs(seed: int = 0) -> dict:
    keys = jax.random.split(jax.random.key(seed), 6)
    return {
        "inputs": noise(keys[0], (GROUPS, TIME, CIN), 1.0, 6.0, ((0, 4), (1, 8))),
        "conv_weight": draw_conv_weight(jax.random.fold_in(keys[5], 71), 0),
        "conv_bias": noise(keys[2], (FEAT,), 0.5, 3.0, (), jnp.float32),
        "labels": plant((jax.random.randint(keys[3], (GROUPS, TIME, LABELS), 0, 4) < 1).astype(jnp.int32), jax.random.fold_in(keys[3], 1), 0, 1),
        "rec_span": draw_rec_span(jax.random.fold_in(keys[5], 71), 0),
    }


RIDGE = 0.1

def stack_taps(stream, before, frames_after):
    half_width = TAPS // 2
    shard_rows = stream.shape[0]
    padded = jnp.pad(stream, ((half_width, half_width), (0, 0)))
    pieces = []
    for tap_index in range(TAPS):
        offset = tap_index - half_width
        shifted = padded[tap_index:tap_index + shard_rows]
        if offset < 0:
            keep_mask = before >= -offset
        elif offset > 0:
            keep_mask = frames_after >= offset
        else:
            keep_mask = before >= 0
        pieces.append(jnp.where(keep_mask[:, None], shifted, jnp.zeros_like(shifted)))
    return jnp.concatenate(pieces, axis=1)

def reference(inputs, conv_weight, conv_bias, labels, rec_span):
    flat_weight = conv_weight.reshape(TAPS * CIN, FEAT)

    def one_group(packed):
        stream, label_rows, before, frames_after = packed
        stacked = stack_taps(stream, before, frames_after)
        pre_act = jnp.dot(stacked.astype(jnp.float32), flat_weight.astype(jnp.float32), preferred_element_type=jnp.float32) + conv_bias
        group_feats = jax.nn.gelu(pre_act, approximate=False).astype(jnp.bfloat16)
        joined = jnp.concatenate([group_feats, label_rows.astype(jnp.bfloat16)], axis=1)
        moments = jnp.dot(group_feats.T.astype(jnp.float32), joined.astype(jnp.float32), preferred_element_type=jnp.float32)
        totals = lax.optimization_barrier(jnp.sum(joined.astype(jnp.float32), axis=0))
        return (group_feats, moments, totals)
    features, moments, totals = lax.map(one_group, (inputs, labels, rec_span[0], rec_span[1]))
    moments = lax.optimization_barrier(jnp.sum(moments, axis=0))
    totals = lax.optimization_barrier(jnp.sum(totals, axis=0))
    frame_count = jnp.float32(FRAMES)
    feat_totals = totals[:FEAT]
    label_totals = totals[FEAT:]
    covariance = (moments[:, :FEAT] - feat_totals[:, None] * feat_totals[None, :] / frame_count) / frame_count
    covariance = covariance + RIDGE * jnp.eye(FEAT, dtype=jnp.float32)
    cross_terms = (moments[:, FEAT:] - feat_totals[:, None] * label_totals[None, :] / frame_count) / jnp.sqrt(frame_count)
    factor = jnp.linalg.cholesky(covariance)
    probe_weights = jax.scipy.linalg.cho_solve((factor, True), cross_terms)
    return (features, probe_weights)
```

```python
import math
import jax
import jax.numpy as jnp
from jax import lax
from jax.experimental import pallas as pl
from jax.experimental.pallas import tpu as pltpu
from jax.sharding import PartitionSpec as P

RIDGE = 0.1
TILE = 128
HI = lax.Precision.HIGHEST
GROUP = 16

def mm(a, b):
    return jnp.dot(a, b, precision=HI, preferred_element_type=jnp.float32)

def mtm(a, b):
    return lax.dot_general(a, b, (((0,), (0,)), ((), ())), precision=HI, preferred_element_type=jnp.float32)

def spread(row, width):
    return jnp.broadcast_to(row, (8, width))

def tree(terms):
    while len(terms) > 1:
        terms = [terms[i] + terms[i + 1] if i + 1 < len(terms) else terms[i] for i in range(0, len(terms), 2)]
    return terms[0]

def invert_tile(slabs):
    count = len(slabs)
    width = 8 * count
    lane = lax.broadcasted_iota(jnp.int32, (8, width), 1)
    sub = lax.broadcasted_iota(jnp.int32, (8, width), 0)
    homes = GROUP // 8
    zero = jnp.zeros((8, width), jnp.float32)
    for j in range(0, width, GROUP):
        first = j // 8
        in_group = (lane >= j) & (lane < j + GROUP)
        near = list(range(first, min(count, first + 2 * homes)))
        cols = {i: [jnp.broadcast_to(slabs[i][:, j + b:j + b + 1], (8, width)) for b in range(GROUP)] for i in near}
        hc = [list(cols[first + t]) for t in range(homes)]
        u = [jnp.where(in_group, jnp.where(lane - sub == j + 8 * t, 1.0, 0.0), slabs[first + t]) for t in range(homes)]
        scale = [jnp.ones((8, width), jnp.float32)] * homes
        for p in range(GROUP):
            h, s = p // 8, p % 8
            r = 1.0 / spread(hc[h][p][s:s + 1], width)
            m = [jnp.where(sub == s, 0.0, hc[t][p]) if t == h else hc[t][p] for t in range(homes)]
            for b in range(p + 1, GROUP):
                f = spread(hc[h][b][s:s + 1], width) * r
                for t in range(homes):
                    hc[t][b] = hc[t][b] - m[t] * f
            row = spread(u[h][s:s + 1], width) * r
            for t in range(homes):
                u[t] = u[t] - m[t] * row
            scale[h] = jnp.where(sub == s, r, scale[h])
        u = [u[t] * scale[t] for t in range(homes)]
        fresh = list(slabs)
        for t in range(homes):
            fresh[first + t] = u[t]
        nxt = near[homes:]
        if nxt:
            rows = [spread(u[b // 8][b % 8:b % 8 + 1], width) for b in range(GROUP)]
            for i in nxt:
                fresh[i] = jnp.where(in_group, 0.0, slabs[i]) - tree([cols[i][b] * rows[b] for b in range(GROUP)])
        left = jnp.concatenate(slabs, axis=0)
        right = jnp.concatenate([u[i - first] if first <= i < first + homes else zero for i in range(count)], axis=0)
        prod = mm(left, right)
        for i in range(count):
            if i not in near:
                fresh[i] = jnp.where(in_group, 0.0, slabs[i]) - prod[8 * i:8 * i + 8]
        slabs = fresh
    return slabs

def factor(a_ref, inv_ref, w_ref, tile):
    size = a_ref.shape[0]
    n = size // tile
    def step(k, carry):
        at = pl.multiple_of(k * tile, tile)
        slabs = [a_ref[pl.ds(at + 8 * i, 8), pl.ds(at, tile)] for i in range(tile // 8)]
        for i, s in enumerate(invert_tile(slabs)):
            inv_ref[pl.ds(at + 8 * i, 8), :] = s
        for c in range(n - 1):
            @pl.when(k == c)
            def _():
                lo, hi = c * tile, (c + 1) * tile
                row = a_ref[lo:hi, hi:]
                w = mm(inv_ref[lo:hi, :], row)
                w_ref[lo:hi, hi:] = w
                for i in range(c + 1, n):
                    s = slice(i * tile, (i + 1) * tile)
                    a_ref[s, i * tile:] -= mtm(a_ref[lo:hi, s], w[:, (i - c - 1) * tile:])
        return carry
    lax.fori_loop(0, n, step, 0)

def substitute(a_ref, inv_ref, w_ref, x_ref, y_ref, tile):
    size = a_ref.shape[0]
    n = size // tile
    for k in range(n):
        lo, hi = k * tile, (k + 1) * tile
        if k:
            x = x_ref[lo:hi, :] - mtm(w_ref[:lo, lo:hi], y_ref[:lo, :])
        else:
            x = x_ref[lo:hi, :]
        y_ref[lo:hi, :] = x
    for k in reversed(range(n)):
        lo, hi = k * tile, (k + 1) * tile
        y = mm(inv_ref[lo:hi, :], y_ref[lo:hi, :])
        if k < n - 1:
            y = y - mm(w_ref[lo:hi, hi:], y_ref[hi:, :])
        y_ref[lo:hi, :] = y


def bits_of(axis, size):
    return [(axis, 1 << i) for i in range(size.bit_length() - 1)]


class Stream:
    def __init__(self, stages, src, out, inbox, sems):
        self.stages, self.src, self.out, self.inbox, self.sems = stages, src, out, inbox, sems
        self.lo, self.length, self.at, self.used = 0, out.shape[0], 0, 0
        self.held, self.copy = (src, 0), None

    def done(self):
        return self.at == 2 * len(self.stages)

    def start(self):
        count = len(self.stages)
        down = self.at < count
        axis, step = self.stages[self.at if down else 2 * count - 1 - self.at]
        me = lax.axis_index(axis)
        self.bit = lax.rem(me // step, 2)
        peer = me + (1 - 2 * self.bit) * step
        if down:
            half = self.length // 2
            ref, base = self.held
            src = ref.at[pl.ds(base + (1 - self.bit) * half, half)]
            dst = self.inbox.at[pl.ds(self.used, half)]
        else:
            src = dst = self.out.at[pl.ds(self.lo, self.length)]
        self.copy = pltpu.make_async_remote_copy(
            src_ref=src, dst_ref=dst,
            send_sem=self.sems.at[0, self.at], recv_sem=self.sems.at[1, self.at],
            device_id={axis: peer}, device_id_type=pl.DeviceIdType.MESH,
        )
        self.copy.start()

    def finish(self):
        self.copy.wait()
        if self.at < len(self.stages):
            half = self.length // 2
            ref, base = self.held
            total = ref[pl.ds(base + self.bit * half, half)] + self.inbox[pl.ds(self.used, half)]
            self.lo, self.length = self.lo + self.bit * half, half
            if self.at < len(self.stages) - 1:
                self.inbox[pl.ds(self.used, half)] = total
                self.held = (self.inbox, self.used)
            else:
                self.out[pl.ds(self.lo, half)] = total
            self.used += half
        else:
            self.lo, self.length = self.lo - self.bit * self.length, 2 * self.length
        self.at += 1


def greet(stages):
    barrier = pltpu.get_barrier_semaphore()
    for axis, step in stages:
        me = lax.axis_index(axis)
        peer = me + (1 - 2 * lax.rem(me // step, 2)) * step
        pl.semaphore_signal(barrier, inc=1, device_id={axis: peer}, device_id_type=pl.DeviceIdType.MESH)
    pl.semaphore_wait(barrier, len(stages))


def orders(frame_size, rec_size):
    frame, rec = bits_of("frame", frame_size), bits_of("rec", rec_size)
    return rec + frame, rec[:1] + frame + rec[1:]


def reduce_kernel(sizes, g_in, x_in, g_out, x_out, g_box, x_box, g_sem, x_sem):
    one, two = orders(*sizes)
    greet(one)
    streams = [Stream(one, g_in, g_out, g_box, g_sem), Stream(two, x_in, x_out, x_box, x_sem)]
    for s in streams:
        s.start()
    while not all(s.done() for s in streams):
        for s in streams:
            if not s.done():
                s.finish()
                if not s.done():
                    s.start()


def reduce_all(g, x):
    sizes = (lax.axis_size("frame"), lax.axis_size("rec"))
    count = len(orders(*sizes)[0])
    vmem = pl.BlockSpec(memory_space=pltpu.VMEM)
    return pl.pallas_call(
        lambda *refs: reduce_kernel(sizes, *refs),
        out_shape=[jax.ShapeDtypeStruct(v.shape, v.dtype) for v in (g, x)],
        in_specs=[vmem, vmem],
        out_specs=[vmem, vmem],
        scratch_shapes=[
            pltpu.VMEM(g.shape, jnp.float32),
            pltpu.VMEM(x.shape, jnp.float32),
            pltpu.SemaphoreType.DMA((2, 2 * count)),
            pltpu.SemaphoreType.DMA((2, 2 * count)),
        ],
        compiler_params=pltpu.CompilerParams(collective_id=0, has_side_effects=True),
    )(g, x)


def pairs(n):
    return [(i, j) for i in range(n) for j in range(i, n)]


def tile_at(ref, slot):
    units = TILE // 8
    return ref[slot * units:(slot + 1) * units].reshape(TILE, TILE)


def column(totals, i):
    return jnp.broadcast_to(totals[i:i + 1], (TILE, TILE)).T


def solve_kernel(frames, g_ref, x_ref, y_ref, a_ref, inv_ref, w_ref, c_ref):
    size, n = a_ref.shape[0], a_ref.shape[0] // TILE
    m = y_ref.shape[1] // TILE
    units = TILE // 8
    rows = -(-(n + m) // 8)
    first = len(pairs(n)) * units
    totals = g_ref[first:first + rows].reshape(8 * rows, TILE)
    cols = [column(totals, i) for i in range(n)]
    eye = lax.broadcasted_iota(jnp.int32, (TILE, TILE), 0) == lax.broadcasted_iota(jnp.int32, (TILE, TILE), 1)
    for slot, (i, j) in enumerate(pairs(n)):
        v = (tile_at(g_ref, slot) - cols[i] * totals[j:j + 1] / frames) / frames
        if i == j:
            v = v + jnp.where(eye, RIDGE, 0.0)
        a_ref[i * TILE:(i + 1) * TILE, j * TILE:(j + 1) * TILE] = v
    factor(a_ref, inv_ref, w_ref, TILE)
    for i in range(n):
        for j in range(m):
            v = tile_at(x_ref, i * m + j) - cols[i] * totals[n + j:n + j + 1] / frames
            c_ref[i * TILE:(i + 1) * TILE, j * TILE:(j + 1) * TILE] = v / math.sqrt(frames)
    substitute(a_ref, inv_ref, w_ref, c_ref, y_ref, TILE)


def solve(g, x, size, wide, frames):
    vmem = pl.BlockSpec(memory_space=pltpu.VMEM)
    return pl.pallas_call(
        lambda *refs: solve_kernel(frames, *refs),
        out_shape=jax.ShapeDtypeStruct((size, wide), jnp.float32),
        in_specs=[vmem, vmem],
        out_specs=vmem,
        scratch_shapes=[
            pltpu.VMEM((size, size), jnp.float32),
            pltpu.VMEM((size, TILE), jnp.float32),
            pltpu.VMEM((size, size), jnp.float32),
            pltpu.VMEM((size, wide), jnp.float32),
        ],
    )(g, x)


def pad_units(v, devices):
    extra = -v.shape[0] % devices
    return jnp.pad(v, ((0, extra), (0, 0), (0, 0)))


def padded_2(shard, sides, width):
    for axis, dim in sides:
        size, length = (lax.axis_size(axis), shard.shape[dim])
        up = [(i, (i + 1) % size) for i in range(size - 1)]
        down = [(j, i) for i, j in up]
        last = lax.slice_in_dim(shard, length - width, length, axis=dim)
        leading = lax.slice_in_dim(shard, 0, width, axis=dim)
        before = lax.ppermute(last, axis, up)
        after = lax.ppermute(leading, axis, down)
        shard = jnp.concatenate([before, shard, after], axis=dim)
    return shard


def per_device(inputs, conv_weight, conv_bias, labels, rec_span):
    tap_count = conv_weight.shape[0]
    half_width = tap_count // 2
    shard_rows = inputs.shape[1]
    feat_width = conv_weight.shape[2]
    padded = padded_2(inputs, (("frame", 1),), half_width)
    before = rec_span[0, 0]
    frames_after = rec_span[1, 0]
    pieces = []
    for tap_index in range(tap_count):
        offset = tap_index - half_width
        shifted = padded[0, tap_index : tap_index + shard_rows]
        if offset < 0:
            keep_mask = before >= -offset
        elif offset > 0:
            keep_mask = frames_after >= offset
        else:
            keep_mask = before >= 0
        pieces.append(jnp.where(keep_mask[:, None], shifted, jnp.zeros_like(shifted)))
    stacked = jnp.concatenate(pieces, axis=1)
    flat_weight = conv_weight.reshape(tap_count * conv_weight.shape[1], feat_width)
    pre_act = jnp.dot(stacked, flat_weight, preferred_element_type=jnp.float32) + conv_bias
    features = jax.nn.gelu(pre_act, approximate=False).astype(jnp.bfloat16)
    joined = jnp.concatenate([features, labels[0].astype(jnp.bfloat16)], axis=1)
    moments = lax.dot_general(
        features, joined, (((0,), (0,)), ((), ())), preferred_element_type=jnp.float32
    )
    totals = jnp.sum(joined, axis=0, dtype=jnp.float32)
    devices = lax.axis_size("frame") * lax.axis_size("rec")
    frames = float(shard_rows * devices)
    wide = labels.shape[2]
    n, m = feat_width // TILE, wide // TILE
    blocks = moments.reshape(n, TILE, n + m, TILE).transpose(0, 2, 1, 3)
    gram = jnp.concatenate([blocks[i, i:n].reshape(-1, 8, TILE) for i in range(n)])
    sums = totals.reshape(n + m, TILE)
    sums = jnp.pad(sums, ((0, -(n + m) % 8), (0, 0))).reshape(-1, 8, TILE)
    g = pad_units(jnp.concatenate([gram, sums]), devices)
    x = pad_units(blocks[:, n:].reshape(-1, 8, TILE), devices)
    g, x = reduce_all(g, x)
    return (features[None], solve(g, x, feat_width, wide, frames))


def solution(mesh):
    in_specs = (P("rec", "frame", None), P(), P(), P("rec", "frame", None), P(None, "rec", "frame"))
    out_specs = (P("rec", "frame", None), P())
    return jax.shard_map(
        per_device, mesh=mesh, in_specs=in_specs, out_specs=out_specs, check_vma=False
    )
```

```python
import math
import jax
import jax.numpy as jnp
from jax import lax
from jax.experimental import pallas as pl
from jax.experimental.pallas import tpu as pltpu
from jax.sharding import PartitionSpec as P

RIDGE = 0.1
TILE = 128
HI = lax.Precision.HIGHEST
GROUP = 16
HALO = 16
STEP = 256

def mm(a, b):
    return jnp.dot(a, b, precision=HI, preferred_element_type=jnp.float32)

def mtm(a, b):
    return lax.dot_general(a, b, (((0,), (0,)), ((), ())), precision=HI, preferred_element_type=jnp.float32)

def spread(row, width):
    return jnp.broadcast_to(row, (8, width))

def tree(terms):
    while len(terms) > 1:
        terms = [terms[i] + terms[i + 1] if i + 1 < len(terms) else terms[i] for i in range(0, len(terms), 2)]
    return terms[0]

def invert_tile(slabs):
    count = len(slabs)
    width = 8 * count
    lane = lax.broadcasted_iota(jnp.int32, (8, width), 1)
    sub = lax.broadcasted_iota(jnp.int32, (8, width), 0)
    homes = GROUP // 8
    zero = jnp.zeros((8, width), jnp.float32)
    for j in range(0, width, GROUP):
        first = j // 8
        in_group = (lane >= j) & (lane < j + GROUP)
        near = list(range(first, min(count, first + 2 * homes)))
        cols = {i: [jnp.broadcast_to(slabs[i][:, j + b:j + b + 1], (8, width)) for b in range(GROUP)] for i in near}
        hc = [list(cols[first + t]) for t in range(homes)]
        u = [jnp.where(in_group, jnp.where(lane - sub == j + 8 * t, 1.0, 0.0), slabs[first + t]) for t in range(homes)]
        scale = [jnp.ones((8, width), jnp.float32)] * homes
        for p in range(GROUP):
            h, s = p // 8, p % 8
            r = 1.0 / spread(hc[h][p][s:s + 1], width)
            m = [jnp.where(sub == s, 0.0, hc[t][p]) if t == h else hc[t][p] for t in range(homes)]
            for b in range(p + 1, GROUP):
                f = spread(hc[h][b][s:s + 1], width) * r
                for t in range(homes):
                    hc[t][b] = hc[t][b] - m[t] * f
            row = spread(u[h][s:s + 1], width) * r
            for t in range(homes):
                u[t] = u[t] - m[t] * row
            scale[h] = jnp.where(sub == s, r, scale[h])
        u = [u[t] * scale[t] for t in range(homes)]
        fresh = list(slabs)
        for t in range(homes):
            fresh[first + t] = u[t]
        nxt = near[homes:]
        if nxt:
            rows = [spread(u[b // 8][b % 8:b % 8 + 1], width) for b in range(GROUP)]
            for i in nxt:
                fresh[i] = jnp.where(in_group, 0.0, slabs[i]) - tree([cols[i][b] * rows[b] for b in range(GROUP)])
        left = jnp.concatenate(slabs, axis=0)
        right = jnp.concatenate([u[i - first] if first <= i < first + homes else zero for i in range(count)], axis=0)
        prod = mm(left, right)
        for i in range(count):
            if i not in near:
                fresh[i] = jnp.where(in_group, 0.0, slabs[i]) - prod[8 * i:8 * i + 8]
        slabs = fresh
    return slabs

def factor(a_ref, inv_ref, w_ref, tile):
    size = a_ref.shape[0]
    n = size // tile
    def step(k, carry):
        at = pl.multiple_of(k * tile, tile)
        slabs = [a_ref[pl.ds(at + 8 * i, 8), pl.ds(at, tile)] for i in range(tile // 8)]
        for i, s in enumerate(invert_tile(slabs)):
            inv_ref[pl.ds(at + 8 * i, 8), :] = s
        for c in range(n - 1):
            @pl.when(k == c)
            def _():
                lo, hi = c * tile, (c + 1) * tile
                row = a_ref[lo:hi, hi:]
                w = mm(inv_ref[lo:hi, :], row)
                w_ref[lo:hi, hi:] = w
                for i in range(c + 1, n):
                    s = slice(i * tile, (i + 1) * tile)
                    a_ref[s, i * tile:] -= mtm(a_ref[lo:hi, s], w[:, (i - c - 1) * tile:])
        return carry
    lax.fori_loop(0, n, step, 0)

def substitute(a_ref, inv_ref, w_ref, x_ref, y_ref, tile):
    size = a_ref.shape[0]
    n = size // tile
    for k in range(n):
        lo, hi = k * tile, (k + 1) * tile
        if k:
            x = x_ref[lo:hi, :] - mtm(w_ref[:lo, lo:hi], y_ref[:lo, :])
        else:
            x = x_ref[lo:hi, :]
        y_ref[lo:hi, :] = x
    for k in reversed(range(n)):
        lo, hi = k * tile, (k + 1) * tile
        y = mm(inv_ref[lo:hi, :], y_ref[lo:hi, :])
        if k < n - 1:
            y = y - mm(w_ref[lo:hi, hi:], y_ref[hi:, :])
        y_ref[lo:hi, :] = y


def bits_of(axis, size):
    return [(axis, 1 << i) for i in range(size.bit_length() - 1)]


class Stream:
    def __init__(self, stages, src, out, inbox, sems):
        self.stages, self.src, self.out, self.inbox, self.sems = stages, src, out, inbox, sems
        self.lo, self.length, self.at, self.used = 0, out.shape[0], 0, 0
        self.held, self.copy = (src, 0), None

    def done(self):
        return self.at == 2 * len(self.stages)

    def start(self):
        count = len(self.stages)
        down = self.at < count
        axis, step = self.stages[self.at if down else 2 * count - 1 - self.at]
        me = lax.axis_index(axis)
        self.bit = lax.rem(me // step, 2)
        peer = me + (1 - 2 * self.bit) * step
        if down:
            half = self.length // 2
            ref, base = self.held
            src = ref.at[pl.ds(base + (1 - self.bit) * half, half)]
            dst = self.inbox.at[pl.ds(self.used, half)]
        else:
            src = dst = self.out.at[pl.ds(self.lo, self.length)]
        self.copy = pltpu.make_async_remote_copy(
            src_ref=src, dst_ref=dst,
            send_sem=self.sems.at[0, self.at], recv_sem=self.sems.at[1, self.at],
            device_id={axis: peer}, device_id_type=pl.DeviceIdType.MESH,
        )
        self.copy.start()

    def finish(self):
        self.copy.wait()
        if self.at < len(self.stages):
            half = self.length // 2
            ref, base = self.held
            total = ref[pl.ds(base + self.bit * half, half)] + self.inbox[pl.ds(self.used, half)]
            self.lo, self.length = self.lo + self.bit * half, half
            if self.at < len(self.stages) - 1:
                self.inbox[pl.ds(self.used, half)] = total
                self.held = (self.inbox, self.used)
            else:
                self.out[pl.ds(self.lo, half)] = total
            self.used += half
        else:
            self.lo, self.length = self.lo - self.bit * self.length, 2 * self.length
        self.at += 1


def greet(stages):
    barrier = pltpu.get_barrier_semaphore()
    for axis, step in stages:
        me = lax.axis_index(axis)
        peer = me + (1 - 2 * lax.rem(me // step, 2)) * step
        pl.semaphore_signal(barrier, inc=1, device_id={axis: peer}, device_id_type=pl.DeviceIdType.MESH)
    pl.semaphore_wait(barrier, len(stages))


def orders(frame_size, rec_size):
    frame, rec = bits_of("frame", frame_size), bits_of("rec", rec_size)
    return rec + frame, rec[:1] + frame + rec[1:]


def reduce_kernel(sizes, g_in, x_in, g_out, x_out, g_box, x_box, g_sem, x_sem):
    one, two = orders(*sizes)
    greet(one)
    streams = [Stream(one, g_in, g_out, g_box, g_sem), Stream(two, x_in, x_out, x_box, x_sem)]
    for s in streams:
        s.start()
    while not all(s.done() for s in streams):
        for s in streams:
            if not s.done():
                s.finish()
                if not s.done():
                    s.start()


def reduce_all(g, x):
    sizes = (lax.axis_size("frame"), lax.axis_size("rec"))
    count = len(orders(*sizes)[0])
    vmem = pl.BlockSpec(memory_space=pltpu.VMEM)
    return pl.pallas_call(
        lambda *refs: reduce_kernel(sizes, *refs),
        out_shape=[jax.ShapeDtypeStruct(v.shape, v.dtype) for v in (g, x)],
        in_specs=[vmem, vmem],
        out_specs=[vmem, vmem],
        scratch_shapes=[
            pltpu.VMEM(g.shape, jnp.float32),
            pltpu.VMEM(x.shape, jnp.float32),
            pltpu.SemaphoreType.DMA((2, 2 * count)),
            pltpu.SemaphoreType.DMA((2, 2 * count)),
        ],
        compiler_params=pltpu.CompilerParams(collective_id=0, has_side_effects=True),
    )(g, x)


def pairs(n):
    return [(i, j) for i in range(n) for j in range(i, n)]


def tile_at(ref, slot):
    units = TILE // 8
    return ref[slot * units:(slot + 1) * units].reshape(TILE, TILE)


def column(totals, i):
    return jnp.broadcast_to(totals[i:i + 1], (TILE, TILE)).T


def solve_kernel(frames, g_ref, x_ref, y_ref, a_ref, inv_ref, w_ref, c_ref):
    size, n = a_ref.shape[0], a_ref.shape[0] // TILE
    m = y_ref.shape[1] // TILE
    units = TILE // 8
    rows = -(-(n + m) // 8)
    first = len(pairs(n)) * units
    totals = g_ref[first:first + rows].reshape(8 * rows, TILE)
    cols = [column(totals, i) for i in range(n)]
    eye = lax.broadcasted_iota(jnp.int32, (TILE, TILE), 0) == lax.broadcasted_iota(jnp.int32, (TILE, TILE), 1)
    for slot, (i, j) in enumerate(pairs(n)):
        v = (tile_at(g_ref, slot) - cols[i] * totals[j:j + 1] / frames) / frames
        if i == j:
            v = v + jnp.where(eye, RIDGE, 0.0)
        a_ref[i * TILE:(i + 1) * TILE, j * TILE:(j + 1) * TILE] = v
    factor(a_ref, inv_ref, w_ref, TILE)
    for i in range(n):
        for j in range(m):
            v = tile_at(x_ref, i * m + j) - cols[i] * totals[n + j:n + j + 1] / frames
            c_ref[i * TILE:(i + 1) * TILE, j * TILE:(j + 1) * TILE] = v / math.sqrt(frames)
    substitute(a_ref, inv_ref, w_ref, c_ref, y_ref, TILE)


def solve(g, x, size, wide, frames):
    vmem = pl.BlockSpec(memory_space=pltpu.VMEM)
    return pl.pallas_call(
        lambda *refs: solve_kernel(frames, *refs),
        out_shape=jax.ShapeDtypeStruct((size, wide), jnp.float32),
        in_specs=[vmem, vmem],
        out_specs=vmem,
        scratch_shapes=[
            pltpu.VMEM((size, size), jnp.float32),
            pltpu.VMEM((size, TILE), jnp.float32),
            pltpu.VMEM((size, size), jnp.float32),
            pltpu.VMEM((size, wide), jnp.float32),
        ],
    )(g, x)


def front_kernel(size, step, x_hbm, w_hbm, bias_ref, lab_hbm, span_ref, feat_hbm, g_ref, x_ref,
                 xb, xf, w, lab, mask, feat, totals, in_sem, halo_sem):
    rows, cin = x_hbm.shape[1], x_hbm.shape[2]
    taps, width = w_hbm.shape[0], w_hbm.shape[2]
    half = taps // 2
    chunks = cin // TILE
    me = lax.axis_index("frame")
    up, down = lax.rem(me + 1, size), lax.rem(me + size - 1, size)
    barrier = pltpu.get_barrier_semaphore()
    for peer in (up, down):
        pl.semaphore_signal(barrier, inc=1, device_id={"frame": peer}, device_id_type=pl.DeviceIdType.MESH)
    load_x = pltpu.make_async_copy(x_hbm.at[0], xb.at[pl.ds(HALO, rows)], in_sem.at[0])
    load_x.start()
    load_w = pltpu.make_async_copy(w_hbm, w, in_sem.at[1])
    load_w.start()
    load_l = pltpu.make_async_copy(lab_hbm.at[0], lab, in_sem.at[2])
    load_l.start()
    pl.semaphore_wait(barrier, 2)
    send_up = pltpu.make_async_remote_copy(
        src_ref=x_hbm.at[0, pl.ds(rows - HALO, HALO)], dst_ref=xb.at[pl.ds(0, HALO)],
        send_sem=halo_sem.at[0], recv_sem=halo_sem.at[1], device_id={"frame": up}, device_id_type=pl.DeviceIdType.MESH)
    send_down = pltpu.make_async_remote_copy(
        src_ref=x_hbm.at[0, pl.ds(0, HALO)], dst_ref=xb.at[pl.ds(rows + HALO, HALO)],
        send_sem=halo_sem.at[2], recv_sem=halo_sem.at[3], device_id={"frame": down}, device_id_type=pl.DeviceIdType.MESH)
    send_up.start()
    send_down.start()
    for i in range(rows // TILE):
        for side in range(2):
            line = span_ref[side, 0:1, i * TILE:(i + 1) * TILE].astype(jnp.float32)
            mask[side, i * TILE:(i + 1) * TILE, :] = jnp.broadcast_to(line, (TILE, TILE)).T
    load_x.wait()
    blocks = rows // step

    def widen(lo, count):
        for c in range(chunks):
            xf[c, lo:lo + count, :] = xb[lo:lo + count, c * TILE:(c + 1) * TILE].astype(jnp.float32)
    widen(HALO, rows)
    load_w.wait()
    totals[...] = jnp.zeros_like(totals)

    def block(b):
        at = b * step
        base = HALO + at
        pieces = []
        for k in range(taps):
            off = k - half
            if off == 0:
                pieces.append(xb[base:base + step, :])
                continue
            keep = mask[0 if off < 0 else 1, at:at + step, :] >= abs(off)
            for c in range(chunks):
                v = xf[c, base + off:base + off + step, :]
                pieces.append(jnp.where(keep, v, 0.0).astype(jnp.bfloat16))
        stacked = jnp.concatenate(pieces, axis=1)
        pre = jnp.dot(stacked, w[...].reshape(taps * cin, width), preferred_element_type=jnp.float32) + bias_ref[...]
        out = (0.5 * pre * (1.0 + lax.erf(pre * math.sqrt(0.5)))).astype(jnp.bfloat16)
        feat[at:at + step, :] = out
        totals[...] += jnp.sum(out.astype(jnp.float32).reshape(step // 8, 8, width), axis=0)

    order = list(range(1, blocks - 1)) + [0, blocks - 1]
    for b in order:
        if b == 0:
            send_up.wait()
            send_down.wait()
            widen(0, HALO)
            widen(rows + HALO, HALO)
        block(b)
    save = pltpu.make_async_copy(feat, feat_hbm.at[0], in_sem.at[3])
    save.start()
    load_l.wait()
    n, m = width // TILE, lab.shape[1] // TILE
    tdot = lambda a, b: lax.dot_general(a, b, (((0,), (0,)), ((), ())), preferred_element_type=jnp.float32)
    units = TILE // 8
    f = feat[...]
    slot = 0
    for i in range(n):
        line = tdot(f[:, i * TILE:(i + 1) * TILE], f[:, i * TILE:])
        for j in range(n - i):
            g_ref[slot * units:(slot + 1) * units] = line[:, j * TILE:(j + 1) * TILE].reshape(units, 8, TILE)
            slot += 1
    lf = lab[...]
    cross = tdot(f, lf.astype(jnp.float32).astype(jnp.bfloat16))
    for i in range(n):
        for j in range(m):
            s = i * m + j
            x_ref[s * units:(s + 1) * units] = cross[i * TILE:(i + 1) * TILE, j * TILE:(j + 1) * TILE].reshape(units, 8, TILE)
    ft = jnp.sum(totals[...], axis=0, keepdims=True)
    lt = jnp.sum(lf, axis=0, keepdims=True).astype(jnp.float32)
    at = slot * units
    allt = jnp.concatenate([ft[:, j * TILE:(j + 1) * TILE] for j in range(n)] + [lt[:, j * TILE:(j + 1) * TILE] for j in range(m)], axis=0)
    g_ref[at:at + (n + m) // 8] = allt.reshape((n + m) // 8, 8, TILE)
    g_ref[at + (n + m) // 8:] = jnp.zeros((g_ref.shape[0] - at - (n + m) // 8, 8, TILE), jnp.float32)
    save.wait()

def front(inputs, conv_weight, conv_bias, labels, rec_span):
    size = lax.axis_size("frame")
    devices = size * lax.axis_size("rec")
    rows, cin = inputs.shape[1:]
    taps, _, width = conv_weight.shape
    wide = labels.shape[2]
    n, m = width // TILE, wide // TILE
    units = len(pairs(n)) * 16 + -(-(n + m) // 8)
    units += -units % devices
    vm = pl.BlockSpec(memory_space=pltpu.VMEM)
    hbm = pl.BlockSpec(memory_space=pltpu.HBM)
    return pl.pallas_call(
        lambda *r: front_kernel(size, STEP, *r),
        out_shape=[jax.ShapeDtypeStruct((1, rows, width), jnp.bfloat16), jax.ShapeDtypeStruct((units, 8, TILE), jnp.float32),
                   jax.ShapeDtypeStruct((n * m * 16, 8, TILE), jnp.float32)],
        in_specs=[hbm, hbm, vm, hbm, vm],
        out_specs=[hbm, vm, vm],
        scratch_shapes=[
            pltpu.VMEM((rows + 2 * HALO, cin), jnp.bfloat16),
            pltpu.VMEM((cin // TILE, rows + 2 * HALO, TILE), jnp.float32),
            pltpu.VMEM(conv_weight.shape, jnp.bfloat16),
            pltpu.VMEM((rows, wide), jnp.int32),
            pltpu.VMEM((2, rows, TILE), jnp.float32),
            pltpu.VMEM((rows, width), jnp.bfloat16),
            pltpu.VMEM((8, width), jnp.float32),
            pltpu.SemaphoreType.DMA((4,)),
            pltpu.SemaphoreType.DMA((4,)),
        ],
        compiler_params=pltpu.CompilerParams(collective_id=1, has_side_effects=True, vmem_limit_bytes=60 << 20),
    )(inputs, conv_weight, conv_bias.reshape(1, width), labels, rec_span)


def per_device(inputs, conv_weight, conv_bias, labels, rec_span):
    width, wide = conv_weight.shape[2], labels.shape[2]
    frames = float(inputs.shape[1] * lax.axis_size("frame") * lax.axis_size("rec"))
    features, g, x = front(inputs, conv_weight, conv_bias, labels, rec_span)
    g, x = reduce_all(g, x)
    return (features, solve(g, x, width, wide, frames))


def solution(mesh):
    in_specs = (P("rec", "frame", None), P(), P(), P("rec", "frame", None), P(None, "rec", "frame"))
    out_specs = (P("rec", "frame", None), P())
    return jax.shard_map(
        per_device, mesh=mesh, in_specs=in_specs, out_specs=out_specs, check_vma=False
    )
```

```python
import math
import jax
import jax.numpy as jnp
from jax import lax
from jax.experimental import pallas as pl
from jax.experimental.pallas import tpu as pltpu
from jax.sharding import PartitionSpec as P

RIDGE = 0.1
TILE = 128
HI = lax.Precision.HIGHEST
GROUP = 16
HALO = 16
STEP = 256

def mm(a, b):
    return jnp.dot(a, b, precision=HI, preferred_element_type=jnp.float32)

def mtm(a, b):
    return lax.dot_general(a, b, (((0,), (0,)), ((), ())), precision=HI, preferred_element_type=jnp.float32)

def spread(row, width):
    return jnp.broadcast_to(row, (8, width))

def tree(terms):
    while len(terms) > 1:
        terms = [terms[i] + terms[i + 1] if i + 1 < len(terms) else terms[i] for i in range(0, len(terms), 2)]
    return terms[0]

def invert_tile(slabs):
    count = len(slabs)
    width = 8 * count
    lane = lax.broadcasted_iota(jnp.int32, (8, width), 1)
    sub = lax.broadcasted_iota(jnp.int32, (8, width), 0)
    homes = GROUP // 8
    zero = jnp.zeros((8, width), jnp.float32)
    for j in range(0, width, GROUP):
        first = j // 8
        in_group = (lane >= j) & (lane < j + GROUP)
        near = list(range(first, min(count, first + 2 * homes)))
        cols = {i: [jnp.broadcast_to(slabs[i][:, j + b:j + b + 1], (8, width)) for b in range(GROUP)] for i in near}
        hc = [list(cols[first + t]) for t in range(homes)]
        u = [jnp.where(in_group, jnp.where(lane - sub == j + 8 * t, 1.0, 0.0), slabs[first + t]) for t in range(homes)]
        scale = [jnp.ones((8, width), jnp.float32)] * homes
        for p in range(GROUP):
            h, s = p // 8, p % 8
            r = 1.0 / spread(hc[h][p][s:s + 1], width)
            m = [jnp.where(sub == s, 0.0, hc[t][p]) if t == h else hc[t][p] for t in range(homes)]
            for b in range(p + 1, GROUP):
                f = spread(hc[h][b][s:s + 1], width) * r
                for t in range(homes):
                    hc[t][b] = hc[t][b] - m[t] * f
            row = spread(u[h][s:s + 1], width) * r
            for t in range(homes):
                u[t] = u[t] - m[t] * row
            scale[h] = jnp.where(sub == s, r, scale[h])
        u = [u[t] * scale[t] for t in range(homes)]
        fresh = list(slabs)
        for t in range(homes):
            fresh[first + t] = u[t]
        nxt = near[homes:]
        if nxt:
            rows = [spread(u[b // 8][b % 8:b % 8 + 1], width) for b in range(GROUP)]
            for i in nxt:
                fresh[i] = jnp.where(in_group, 0.0, slabs[i]) - tree([cols[i][b] * rows[b] for b in range(GROUP)])
        left = jnp.concatenate(slabs, axis=0)
        right = jnp.concatenate([u[i - first] if first <= i < first + homes else zero for i in range(count)], axis=0)
        prod = mm(left, right)
        for i in range(count):
            if i not in near:
                fresh[i] = jnp.where(in_group, 0.0, slabs[i]) - prod[8 * i:8 * i + 8]
        slabs = fresh
    return slabs

def factor(a_ref, inv_ref, w_ref, tile):
    size = a_ref.shape[0]
    n = size // tile
    def step(k, carry):
        at = pl.multiple_of(k * tile, tile)
        slabs = [a_ref[pl.ds(at + 8 * i, 8), pl.ds(at, tile)] for i in range(tile // 8)]
        for i, s in enumerate(invert_tile(slabs)):
            inv_ref[pl.ds(at + 8 * i, 8), :] = s
        for c in range(n - 1):
            @pl.when(k == c)
            def _():
                lo, hi = c * tile, (c + 1) * tile
                row = a_ref[lo:hi, hi:]
                w = mm(inv_ref[lo:hi, :], row)
                w_ref[lo:hi, hi:] = w
                for i in range(c + 1, n):
                    s = slice(i * tile, (i + 1) * tile)
                    a_ref[s, i * tile:] -= mtm(a_ref[lo:hi, s], w[:, (i - c - 1) * tile:])
        return carry
    lax.fori_loop(0, n, step, 0)

def substitute(a_ref, inv_ref, w_ref, x_ref, y_ref, tile):
    size = a_ref.shape[0]
    n = size // tile
    for k in range(n):
        lo, hi = k * tile, (k + 1) * tile
        if k:
            x = x_ref[lo:hi, :] - mtm(w_ref[:lo, lo:hi], y_ref[:lo, :])
        else:
            x = x_ref[lo:hi, :]
        y_ref[lo:hi, :] = x
    for k in reversed(range(n)):
        lo, hi = k * tile, (k + 1) * tile
        y = mm(inv_ref[lo:hi, :], y_ref[lo:hi, :])
        if k < n - 1:
            y = y - mm(w_ref[lo:hi, hi:], y_ref[hi:, :])
        y_ref[lo:hi, :] = y


def bits_of(axis, size):
    return [(axis, 1 << i) for i in range(size.bit_length() - 1)]


def pairs(n):
    return [(i, j) for i in range(n) for j in range(i, n)]


def groups_of(sizes, most):
    frame, rec = bits_of("frame", sizes[0]), bits_of("rec", sizes[1])
    rest = rec[1:2] + frame[:1] + frame[1:] + rec[2:]
    return [rec[:1]] + [rest[i:i + most] for i in range(0, len(rest), most)]


def bit_values(group):
    return [lax.rem(lax.axis_index(axis) // step, 2) for axis, step in group]


def peer_of(group, bits, mask):
    place = {}
    for i, (axis, step) in enumerate(group):
        if mask >> i & 1:
            place[axis] = place.get(axis, lax.axis_index(axis)) + (1 - 2 * bits[i]) * step
    return place


def rank_of(bits, mask=0):
    return sum((1 - v if mask >> i & 1 else v) * (1 << i) for i, v in enumerate(bits))


def inbox_units(groups, units):
    total = 0
    for group in groups:
        chunk = units >> len(group)
        total += units - chunk
        units = chunk
    return total


def copies_of(groups):
    return 2 * sum((1 << len(g)) - 1 for g in groups)


class Stream:
    def __init__(self, groups, src, out, acc, inbox, sems):
        self.groups, self.src, self.out, self.acc, self.inbox, self.sems = groups, src, out, acc, inbox, sems
        self.length, self.lo, self.at = src.shape[0], 0, 0
        self.held, self.used, self.kept, self.sem = (src, 0), 0, 0, 0
        self.copies = []

    def done(self):
        return self.at == 2 * len(self.groups)

    def start(self):
        count = len(self.groups)
        self.down = self.at < count
        self.group = self.groups[self.at if self.down else 2 * count - 1 - self.at]
        self.bits = bit_values(self.group)
        self.copies = []
        self.chunk = self.length >> len(self.group)
        for mask in range(1, 1 << len(self.group)):
            if self.down:
                ref, base = self.held
                src = ref.at[pl.ds(base + rank_of(self.bits, mask) * self.chunk, self.chunk)]
                dst = self.inbox.at[pl.ds(self.used + (mask - 1) * self.chunk, self.chunk)]
            else:
                src = dst = self.out.at[pl.ds(self.lo, self.length)]
            copy = pltpu.make_async_remote_copy(
                src_ref=src, dst_ref=dst,
                send_sem=self.sems.at[0, self.sem], recv_sem=self.sems.at[1, self.sem],
                device_id=peer_of(self.group, self.bits, mask), device_id_type=pl.DeviceIdType.MESH,
            )
            copy.start()
            self.copies.append(copy)
            self.sem += 1

    def finish(self):
        for copy in self.copies:
            copy.wait()
        rank = rank_of(self.bits)
        if self.down:
            ref, base = self.held
            total = ref[pl.ds(base + rank * self.chunk, self.chunk)]
            for i in range((1 << len(self.group)) - 1):
                total = total + self.inbox[self.used + i * self.chunk:self.used + (i + 1) * self.chunk]
            self.used += self.length - self.chunk
            self.lo, self.length = self.lo + rank * self.chunk, self.chunk
            if self.at < len(self.groups) - 1:
                self.acc[self.kept:self.kept + self.chunk] = total
                self.held = (self.acc, self.kept)
                self.kept += self.chunk
            else:
                self.out[pl.ds(self.lo, self.chunk)] = total
        else:
            self.lo = self.lo - rank * self.length
            self.length = self.length << len(self.group)
        self.at += 1


def stream_scratch(groups, units):
    held = sum(units >> sum(len(g) for g in groups[:i + 1]) for i in range(len(groups) - 1))
    return [
        pltpu.VMEM((max(held, 1), 8, TILE), jnp.float32),
        pltpu.VMEM((inbox_units(groups, units), 8, TILE), jnp.float32),
        pltpu.SemaphoreType.DMA((2, copies_of(groups))),
    ]


def greet(plans, size):
    barrier = pltpu.get_barrier_semaphore()
    met = {}
    for groups in plans:
        for group in groups:
            for mask in range(1, 1 << len(group)):
                met[tuple(sorted(bit for i, bit in enumerate(group) if mask >> i & 1))] = (group, mask)
    for group, mask in met.values():
        pl.semaphore_signal(barrier, inc=1, device_id=peer_of(group, bit_values(group), mask), device_id_type=pl.DeviceIdType.MESH)
    me = lax.axis_index("frame")
    for peer in (lax.rem(me + 1, size), lax.rem(me + size - 1, size)):
        pl.semaphore_signal(barrier, inc=1, device_id={"frame": peer}, device_id_type=pl.DeviceIdType.MESH)
    return barrier, len(met) + 2


def tile_at(ref, slot):
    units = TILE // 8
    return ref[slot * units:(slot + 1) * units].reshape(TILE, TILE)


def column(totals, i):
    return jnp.broadcast_to(totals[i:i + 1], (TILE, TILE)).T


def solve_kernel(frames, ga_ref, gb_ref, x_ref, y_ref, a_ref, inv_ref, w_ref, c_ref):
    size, n = a_ref.shape[0], a_ref.shape[0] // TILE
    m = y_ref.shape[1] // TILE
    hold = TILE // 2
    head = tile_at(ga_ref, 0)
    sums = head[hold:, :hold]
    totals = jnp.concatenate(
        [jnp.concatenate([sums[2 * i:2 * i + 1], sums[2 * i + 1:2 * i + 2]], axis=1) for i in range(n + m)], axis=0)
    cols = [column(totals, i) for i in range(n)]
    down = lax.broadcasted_iota(jnp.int32, (TILE, TILE), 0)
    across = lax.broadcasted_iota(jnp.int32, (TILE, TILE), 1)
    head = jnp.where(down <= across, head, head.T)
    for i, j in pairs(n):
        if i == 0:
            tile = head if j == 0 else tile_at(ga_ref, j)
        else:
            tile = tile_at(gb_ref, pairs(n).index((i, j)) - n)
        v = (tile - cols[i] * totals[j:j + 1] / frames) / frames
        if i == j:
            v = v + jnp.where(down == across, RIDGE, 0.0)
        a_ref[i * TILE:(i + 1) * TILE, j * TILE:(j + 1) * TILE] = v
    factor(a_ref, inv_ref, w_ref, TILE)
    for i in range(n):
        for j in range(m):
            v = tile_at(x_ref, i * m + j) - cols[i] * totals[n + j:n + j + 1] / frames
            c_ref[i * TILE:(i + 1) * TILE, j * TILE:(j + 1) * TILE] = v / math.sqrt(frames)
    substitute(a_ref, inv_ref, w_ref, c_ref, y_ref, TILE)


def solve(ga, gb, x, size, wide, frames):
    vmem = pl.BlockSpec(memory_space=pltpu.VMEM)
    return pl.pallas_call(
        lambda *refs: solve_kernel(frames, *refs),
        out_shape=jax.ShapeDtypeStruct((size, wide), jnp.float32),
        in_specs=[vmem, vmem, vmem],
        out_specs=vmem,
        scratch_shapes=[
            pltpu.VMEM((size, size), jnp.float32),
            pltpu.VMEM((size, TILE), jnp.float32),
            pltpu.VMEM((size, size), jnp.float32),
            pltpu.VMEM((size, wide), jnp.float32),
        ],
        compiler_params=pltpu.CompilerParams(vmem_limit_bytes=60 << 20),
    )(ga, gb, x)


def front_kernel(sizes, x_hbm, w_hbm, bias_ref, lab_hbm, span_ref, feat_hbm, a_out, b_out, x_out,
                 xb, xf, w, lab, mask, feat, totals, in_sem, halo_sem, a_src, b_src, x_src, *boxes):
    rows, cin = x_hbm.shape[1], x_hbm.shape[2]
    taps, width = w_hbm.shape[0], w_hbm.shape[2]
    half = taps // 2
    chunks = cin // TILE
    size = sizes[0]
    me = lax.axis_index("frame")
    up, down = lax.rem(me + 1, size), lax.rem(me + size - 1, size)
    plans = [groups_of(sizes, 4), groups_of(sizes, 4), groups_of(sizes, 2)]
    barrier, signals = greet(plans, size)
    load_x = pltpu.make_async_copy(x_hbm.at[0], xb.at[pl.ds(HALO, rows)], in_sem.at[0])
    load_x.start()
    load_w = pltpu.make_async_copy(w_hbm, w, in_sem.at[1])
    load_w.start()
    load_l = pltpu.make_async_copy(lab_hbm.at[0], lab, in_sem.at[2])
    load_l.start()
    for i in range(rows // TILE):
        for side in range(2):
            line = span_ref[side, 0:1, i * TILE:(i + 1) * TILE].astype(jnp.float32)
            mask[side, i * TILE:(i + 1) * TILE, :] = jnp.broadcast_to(line, (TILE, TILE)).T
    load_x.wait()

    def widen(lo, count):
        for c in range(chunks):
            xf[c, lo:lo + count, :] = xb[lo:lo + count, c * TILE:(c + 1) * TILE].astype(jnp.float32)
    widen(HALO, rows)
    load_w.wait()
    totals[...] = jnp.zeros_like(totals)

    def taps_at(at, count):
        pieces = []
        for k in range(taps):
            off = k - half
            base = HALO + at
            if off == 0:
                pieces.append(xb[base:base + count, :])
                continue
            keep = mask[0 if off < 0 else 1, at:at + count, :] >= abs(off)
            for c in range(chunks):
                v = xf[c, base + off:base + off + count, :]
                pieces.append(jnp.where(keep, v, 0.0).astype(jnp.bfloat16))
        return jnp.concatenate(pieces, axis=1)

    def block(parts):
        stacked = [taps_at(at, count) for at, count in parts]
        stacked = stacked[0] if len(stacked) == 1 else jnp.concatenate(stacked, axis=0)
        pre = jnp.dot(stacked, w[...].reshape(taps * cin, width), preferred_element_type=jnp.float32) + bias_ref[...]
        out = (0.5 * pre * (1.0 + lax.erf(pre * math.sqrt(0.5)))).astype(jnp.bfloat16)
        done = 0
        for at, count in parts:
            feat[at:at + count, :] = out[done:done + count]
            done += count
        totals[...] += jnp.sum(out.astype(jnp.float32).reshape(-1, 8, width), axis=0)

    cuts = list(range(HALO, rows - HALO, STEP)) + [rows - HALO]
    blocks = list(zip(cuts[:-1], cuts[1:]))
    block([(blocks[0][0], blocks[0][1] - blocks[0][0])])
    pl.semaphore_wait(barrier, signals)
    send_up = pltpu.make_async_remote_copy(
        src_ref=x_hbm.at[0, pl.ds(rows - HALO, HALO)], dst_ref=xb.at[pl.ds(0, HALO)],
        send_sem=halo_sem.at[0], recv_sem=halo_sem.at[1], device_id={"frame": up}, device_id_type=pl.DeviceIdType.MESH)
    send_down = pltpu.make_async_remote_copy(
        src_ref=x_hbm.at[0, pl.ds(0, HALO)], dst_ref=xb.at[pl.ds(rows + HALO, HALO)],
        send_sem=halo_sem.at[2], recv_sem=halo_sem.at[3], device_id={"frame": down}, device_id_type=pl.DeviceIdType.MESH)
    send_up.start()
    send_down.start()
    for lo, hi in blocks[1:]:
        block([(lo, hi - lo)])
    send_up.wait()
    send_down.wait()
    widen(0, HALO)
    widen(rows + HALO, HALO)
    block([(0, HALO), (rows - HALO, HALO)])
    save = pltpu.make_async_copy(feat, feat_hbm.at[0], in_sem.at[3])
    save.start()
    n, m = width // TILE, lab.shape[1] // TILE
    units = TILE // 8

    def tdot(p, q):
        return lax.dot_general(p, q, (((0,), (0,)), ((), ())), preferred_element_type=jnp.float32)

    def put(ref, slot, tile):
        ref[slot * units:(slot + 1) * units] = tile.reshape(units, 8, TILE)

    streams = [
        Stream(plan, src, out, *boxes[3 * i:3 * i + 3])
        for i, (plan, src, out) in enumerate(zip(plans, (a_src, b_src, x_src), (a_out, b_out, x_out)))
    ]
    load_l.wait()
    ft = jnp.sum(totals[...], axis=0, keepdims=True)
    lt = jnp.sum(lab[...], axis=0, keepdims=True).astype(jnp.float32)
    hold = TILE // 2
    sums = [v[:, c:c + hold] for v in (ft, lt) for c in range(0, v.shape[1], hold)]
    line = tdot(feat[:, :TILE], feat[...])
    corner = jnp.concatenate(sums + [jnp.zeros((hold - len(sums), hold), jnp.float32)], axis=0)
    head = line[:, :TILE]
    head = jnp.concatenate([head[:hold], jnp.concatenate([corner, head[hold:, hold:]], axis=1)], axis=0)
    put(a_src, 0, head)
    for j in range(1, n):
        put(a_src, j, line[:, j * TILE:(j + 1) * TILE])
    if a_src.shape[0] > n * units:
        a_src[n * units:] = jnp.zeros((a_src.shape[0] - n * units, 8, TILE), jnp.float32)
    streams[0].start()
    slot = 0
    for i in range(1, n):
        line = tdot(feat[:, i * TILE:(i + 1) * TILE], feat[:, i * TILE:])
        for j in range(n - i):
            put(b_src, slot, line[:, j * TILE:(j + 1) * TILE])
            slot += 1
    if b_src.shape[0] > slot * units:
        b_src[slot * units:] = jnp.zeros((b_src.shape[0] - slot * units, 8, TILE), jnp.float32)
    streams[1].start()
    cross = tdot(feat[...], lab[...].astype(jnp.float32).astype(jnp.bfloat16))
    for i in range(n):
        for j in range(m):
            put(x_src, i * m + j, cross[i * TILE:(i + 1) * TILE, j * TILE:(j + 1) * TILE])
    if x_src.shape[0] > n * m * units:
        x_src[n * m * units:] = jnp.zeros((x_src.shape[0] - n * m * units, 8, TILE), jnp.float32)
    streams[2].start()
    while not all(s.done() for s in streams):
        for s in streams:
            if not s.done():
                s.finish()
                if not s.done():
                    s.start()
    save.wait()


def front(inputs, conv_weight, conv_bias, labels, rec_span):
    sizes = (lax.axis_size("frame"), lax.axis_size("rec"))
    devices = sizes[0] * sizes[1]
    rows, cin = inputs.shape[1:]
    taps, _, width = conv_weight.shape
    wide = labels.shape[2]
    n, m = width // TILE, wide // TILE
    tiles = [n, n * (n - 1) // 2, n * m]
    units = [-(-t * (TILE // 8) // devices) * devices for t in tiles]
    vm = pl.BlockSpec(memory_space=pltpu.VMEM)
    hbm = pl.BlockSpec(memory_space=pltpu.HBM)
    plans = [groups_of(sizes, 4), groups_of(sizes, 4), groups_of(sizes, 2)]
    boxes = [v for plan, u in zip(plans, units) for v in stream_scratch(plan, u)]
    return pl.pallas_call(
        lambda *r: front_kernel(sizes, *r),
        out_shape=[jax.ShapeDtypeStruct((1, rows, width), jnp.bfloat16)]
        + [jax.ShapeDtypeStruct((u, 8, TILE), jnp.float32) for u in units],
        in_specs=[hbm, hbm, vm, hbm, vm],
        out_specs=[hbm, vm, vm, vm],
        scratch_shapes=[
            pltpu.VMEM((rows + 2 * HALO, cin), jnp.bfloat16),
            pltpu.VMEM((cin // TILE, rows + 2 * HALO, TILE), jnp.float32),
            pltpu.VMEM(conv_weight.shape, jnp.bfloat16),
            pltpu.VMEM((rows, wide), jnp.int32),
            pltpu.VMEM((2, rows, TILE), jnp.float32),
            pltpu.VMEM((rows, width), jnp.bfloat16),
            pltpu.VMEM((8, width), jnp.float32),
            pltpu.SemaphoreType.DMA((4,)),
            pltpu.SemaphoreType.DMA((4,)),
        ] + [pltpu.VMEM((u, 8, TILE), jnp.float32) for u in units] + boxes,
        compiler_params=pltpu.CompilerParams(collective_id=0, has_side_effects=True, vmem_limit_bytes=60 << 20),
    )(inputs, conv_weight, conv_bias.reshape(1, width), labels, rec_span)


def per_device(inputs, conv_weight, conv_bias, labels, rec_span):
    width, wide = conv_weight.shape[2], labels.shape[2]
    frames = float(inputs.shape[1] * lax.axis_size("frame") * lax.axis_size("rec"))
    features, ga, gb, x = front(inputs, conv_weight, conv_bias, labels, rec_span)
    return (features, solve(ga, gb, x, width, wide, frames))


def solution(mesh):
    in_specs = (P("rec", "frame", None), P(), P(), P("rec", "frame", None), P(None, "rec", "frame"))
    out_specs = (P("rec", "frame", None), P())
    return jax.shard_map(
        per_device, mesh=mesh, in_specs=in_specs, out_specs=out_specs, check_vma=False
    )
```

```python
import math
import jax
import jax.numpy as jnp
from jax import lax
from jax.experimental import pallas as pl
from jax.experimental.pallas import tpu as pltpu
from jax.sharding import PartitionSpec as P

RIDGE = 0.1
TILE = 128
HI = lax.Precision.HIGHEST
GROUP = 16
HALO = 16
STEP = 256

def mm(a, b):
    return jnp.dot(a, b, precision=HI, preferred_element_type=jnp.float32)

def mtm(a, b):
    return lax.dot_general(a, b, (((0,), (0,)), ((), ())), precision=HI, preferred_element_type=jnp.float32)

def spread(row, width):
    return jnp.broadcast_to(row, (8, width))

def tree(terms):
    while len(terms) > 1:
        terms = [terms[i] + terms[i + 1] if i + 1 < len(terms) else terms[i] for i in range(0, len(terms), 2)]
    return terms[0]

def invert_tile(slabs):
    count = len(slabs)
    width = 8 * count
    lane = lax.broadcasted_iota(jnp.int32, (8, width), 1)
    sub = lax.broadcasted_iota(jnp.int32, (8, width), 0)
    homes = GROUP // 8
    zero = jnp.zeros((8, width), jnp.float32)
    for j in range(0, width, GROUP):
        first = j // 8
        in_group = (lane >= j) & (lane < j + GROUP)
        near = list(range(first, min(count, first + 2 * homes)))
        cols = {i: [jnp.broadcast_to(slabs[i][:, j + b:j + b + 1], (8, width)) for b in range(GROUP)] for i in near}
        hc = [list(cols[first + t]) for t in range(homes)]
        u = [jnp.where(in_group, jnp.where(lane - sub == j + 8 * t, 1.0, 0.0), slabs[first + t]) for t in range(homes)]
        scale = [jnp.ones((8, width), jnp.float32)] * homes
        for p in range(GROUP):
            h, s = p // 8, p % 8
            r = 1.0 / spread(hc[h][p][s:s + 1], width)
            m = [jnp.where(sub == s, 0.0, hc[t][p]) if t == h else hc[t][p] for t in range(homes)]
            for b in range(p + 1, GROUP):
                f = spread(hc[h][b][s:s + 1], width) * r
                for t in range(homes):
                    hc[t][b] = hc[t][b] - m[t] * f
            row = spread(u[h][s:s + 1], width) * r
            for t in range(homes):
                u[t] = u[t] - m[t] * row
            scale[h] = jnp.where(sub == s, r, scale[h])
        u = [u[t] * scale[t] for t in range(homes)]
        fresh = list(slabs)
        for t in range(homes):
            fresh[first + t] = u[t]
        nxt = near[homes:]
        if nxt:
            rows = [spread(u[b // 8][b % 8:b % 8 + 1], width) for b in range(GROUP)]
            for i in nxt:
                fresh[i] = jnp.where(in_group, 0.0, slabs[i]) - tree([cols[i][b] * rows[b] for b in range(GROUP)])
        left = jnp.concatenate(slabs, axis=0)
        right = jnp.concatenate([u[i - first] if first <= i < first + homes else zero for i in range(count)], axis=0)
        prod = mm(left, right)
        for i in range(count):
            if i not in near:
                fresh[i] = jnp.where(in_group, 0.0, slabs[i]) - prod[8 * i:8 * i + 8]
        slabs = fresh
    return slabs

def invert_block(a_ref, inv_ref, k):
    lo, hi = k * TILE, (k + 1) * TILE
    slabs = invert_tile([a_ref[lo + 8 * i:lo + 8 * i + 8, lo:hi] for i in range(TILE // 8)])
    for i, s in enumerate(slabs):
        inv_ref[lo + 8 * i:lo + 8 * i + 8, :] = s


def scale_row(a_ref, inv_ref, w_ref, k):
    lo, hi = k * TILE, (k + 1) * TILE
    w_ref[lo:hi, hi:] = mm(inv_ref[lo:hi, :], a_ref[lo:hi, hi:])


def update_rest(a_ref, w_ref, k):
    lo, hi = k * TILE, (k + 1) * TILE
    for i in range(k + 1, a_ref.shape[0] // TILE):
        s = slice(i * TILE, (i + 1) * TILE)
        a_ref[s, i * TILE:] -= mtm(a_ref[lo:hi, s], w_ref[lo:hi, i * TILE:])


def substitute(inv_ref, w_ref, x_ref, y_ref, ready):
    n = y_ref.shape[0] // TILE
    for k in range(n):
        lo, hi = k * TILE, (k + 1) * TILE
        x = x_ref[lo:hi, :]
        if k:
            x = x - mtm(w_ref[:lo, lo:hi], y_ref[:lo, :])
        y_ref[lo:hi, :] = x
    for k in reversed(range(n)):
        lo, hi = k * TILE, (k + 1) * TILE
        y = mm(inv_ref[lo:hi, :], y_ref[lo:hi, :])
        if k < n - 1:
            y = y - mm(w_ref[lo:hi, hi:], y_ref[hi:, :])
        y_ref[lo:hi, :] = y
        ready(k)


def bits_of(axis, size):
    return [(axis, 1 << i) for i in range(size.bit_length() - 1)]


def pairs(n):
    return [(i, j) for i in range(n) for j in range(i, n)]


def groups_of(sizes, most):
    frame, rec = bits_of("frame", sizes[0]), bits_of("rec", sizes[1])
    rest = rec[1:2] + frame[:1] + frame[1:] + rec[2:]
    return [rec[:1]] + [rest[i:i + most] for i in range(0, len(rest), most)]


def bit_values(group):
    return [lax.rem(lax.axis_index(axis) // step, 2) for axis, step in group]


def peer_of(group, bits, mask):
    place = {}
    for i, (axis, step) in enumerate(group):
        if mask >> i & 1:
            place[axis] = place.get(axis, lax.axis_index(axis)) + (1 - 2 * bits[i]) * step
    return place


def rank_of(bits, mask=0):
    return sum((1 - v if mask >> i & 1 else v) * (1 << i) for i, v in enumerate(bits))


def inbox_units(groups, units):
    total = 0
    for group in groups:
        chunk = units >> len(group)
        total += units - chunk
        units = chunk
    return total


def copies_of(groups):
    return 2 * sum((1 << len(g)) - 1 for g in groups)


class Stream:
    def __init__(self, groups, src, out, acc, inbox, sems):
        self.groups, self.src, self.out, self.acc, self.inbox, self.sems = groups, src, out, acc, inbox, sems
        self.length, self.lo, self.at = src.shape[0], 0, 0
        self.held, self.used, self.kept, self.sem = (src, 0), 0, 0, 0
        self.copies = []

    def done(self):
        return self.at == 2 * len(self.groups)

    def start(self):
        count = len(self.groups)
        self.down = self.at < count
        self.group = self.groups[self.at if self.down else 2 * count - 1 - self.at]
        self.bits = bit_values(self.group)
        self.copies = []
        self.chunk = self.length >> len(self.group)
        for mask in range(1, 1 << len(self.group)):
            if self.down:
                ref, base = self.held
                src = ref.at[pl.ds(base + rank_of(self.bits, mask) * self.chunk, self.chunk)]
                dst = self.inbox.at[pl.ds(self.used + (mask - 1) * self.chunk, self.chunk)]
            else:
                src = dst = self.out.at[pl.ds(self.lo, self.length)]
            copy = pltpu.make_async_remote_copy(
                src_ref=src, dst_ref=dst,
                send_sem=self.sems.at[0, self.sem], recv_sem=self.sems.at[1, self.sem],
                device_id=peer_of(self.group, self.bits, mask), device_id_type=pl.DeviceIdType.MESH,
            )
            copy.start()
            self.copies.append(copy)
            self.sem += 1

    def finish(self):
        for copy in self.copies:
            copy.wait()
        rank = rank_of(self.bits)
        if self.down:
            ref, base = self.held
            total = ref[pl.ds(base + rank * self.chunk, self.chunk)]
            for i in range((1 << len(self.group)) - 1):
                total = total + self.inbox[self.used + i * self.chunk:self.used + (i + 1) * self.chunk]
            self.used += self.length - self.chunk
            self.lo, self.length = self.lo + rank * self.chunk, self.chunk
            if self.at < len(self.groups) - 1:
                self.acc[self.kept:self.kept + self.chunk] = total
                self.held = (self.acc, self.kept)
                self.kept += self.chunk
            else:
                self.out[pl.ds(self.lo, self.chunk)] = total
        else:
            self.lo = self.lo - rank * self.length
            self.length = self.length << len(self.group)
        self.at += 1


def stream_scratch(groups, units):
    held = sum(units >> sum(len(g) for g in groups[:i + 1]) for i in range(len(groups) - 1))
    return [
        pltpu.VMEM((max(held, 1), 8, TILE), jnp.float32),
        pltpu.VMEM((inbox_units(groups, units), 8, TILE), jnp.float32),
        pltpu.SemaphoreType.DMA((2, copies_of(groups))),
    ]


def greet(plans, size):
    barrier = pltpu.get_barrier_semaphore()
    met = {}
    for groups in plans:
        for group in groups:
            for mask in range(1, 1 << len(group)):
                met[tuple(sorted(bit for i, bit in enumerate(group) if mask >> i & 1))] = (group, mask)
    for group, mask in met.values():
        pl.semaphore_signal(barrier, inc=1, device_id=peer_of(group, bit_values(group), mask), device_id_type=pl.DeviceIdType.MESH)
    me = lax.axis_index("frame")
    for peer in (lax.rem(me + 1, size), lax.rem(me + size - 1, size)):
        pl.semaphore_signal(barrier, inc=1, device_id={"frame": peer}, device_id_type=pl.DeviceIdType.MESH)
    return barrier, len(met) + 2


def tile_at(ref, slot):
    units = TILE // 8
    return ref[slot * units:(slot + 1) * units].reshape(TILE, TILE)


def column(totals, i):
    return jnp.broadcast_to(totals[i:i + 1], (TILE, TILE)).T


class Centre:
    def __init__(self, frames, n, m, head):
        hold = TILE // 2
        sums = head[hold:, :hold]
        self.frames, self.n = frames, n
        self.totals = jnp.concatenate(
            [jnp.concatenate([sums[2 * i:2 * i + 1], sums[2 * i + 1:2 * i + 2]], axis=1) for i in range(n + m)], axis=0)
        self.cols = [column(self.totals, i) for i in range(n)]
        self.down = lax.broadcasted_iota(jnp.int32, (TILE, TILE), 0)
        self.across = lax.broadcasted_iota(jnp.int32, (TILE, TILE), 1)

    def mirror(self, tile):
        return jnp.where(self.down <= self.across, tile, tile.T)

    def gram(self, a_ref, i, j, tile):
        v = (tile - self.cols[i] * self.totals[j:j + 1] / self.frames) / self.frames
        if i == j:
            v = v + jnp.where(self.down == self.across, RIDGE, 0.0)
        a_ref[i * TILE:(i + 1) * TILE, j * TILE:(j + 1) * TILE] = v

    def cross(self, c_ref, i, j, tile):
        v = tile - self.cols[i] * self.totals[self.n + j:self.n + j + 1] / self.frames
        c_ref[i * TILE:(i + 1) * TILE, j * TILE:(j + 1) * TILE] = v / math.sqrt(self.frames)


def front_kernel(sizes, x_hbm, w_hbm, bias_ref, lab_hbm, span_ref, feat_hbm, y_hbm,
                 xb, xf, w, lab, mask, feat, totals, in_sem, halo_sem, out_sem, a_ref, inv_ref, w_ref, c_ref, y_ref,
                 a_src, b_src, x_src, a_out, b_out, x_out, *boxes):
    rows, cin = x_hbm.shape[1], x_hbm.shape[2]
    taps, width = w_hbm.shape[0], w_hbm.shape[2]
    half = taps // 2
    chunks = cin // TILE
    size = sizes[0]
    me = lax.axis_index("frame")
    up, down = lax.rem(me + 1, size), lax.rem(me + size - 1, size)
    plans = [groups_of(sizes, 4), groups_of(sizes, 4), groups_of(sizes, 2)]
    barrier, signals = greet(plans, size)
    load_x = pltpu.make_async_copy(x_hbm.at[0], xb.at[pl.ds(HALO, rows)], in_sem.at[0])
    load_x.start()
    load_w = pltpu.make_async_copy(w_hbm, w, in_sem.at[1])
    load_w.start()
    load_l = pltpu.make_async_copy(lab_hbm.at[0], lab, in_sem.at[2])
    load_l.start()
    for i in range(rows // TILE):
        for side in range(2):
            line = span_ref[side, 0:1, i * TILE:(i + 1) * TILE].astype(jnp.float32)
            mask[side, i * TILE:(i + 1) * TILE, :] = jnp.broadcast_to(line, (TILE, TILE)).T
    load_x.wait()

    def widen(lo, count):
        for c in range(chunks):
            xf[c, lo:lo + count, :] = xb[lo:lo + count, c * TILE:(c + 1) * TILE].astype(jnp.float32)
    widen(HALO, rows)
    load_w.wait()
    totals[...] = jnp.zeros_like(totals)

    def taps_at(at, count):
        pieces = []
        for k in range(taps):
            off = k - half
            base = HALO + at
            if off == 0:
                pieces.append(xb[base:base + count, :])
                continue
            keep = mask[0 if off < 0 else 1, at:at + count, :] >= abs(off)
            for c in range(chunks):
                v = xf[c, base + off:base + off + count, :]
                pieces.append(jnp.where(keep, v, 0.0).astype(jnp.bfloat16))
        return jnp.concatenate(pieces, axis=1)

    def block(parts):
        stacked = [taps_at(at, count) for at, count in parts]
        stacked = stacked[0] if len(stacked) == 1 else jnp.concatenate(stacked, axis=0)
        pre = jnp.dot(stacked, w[...].reshape(taps * cin, width), preferred_element_type=jnp.float32) + bias_ref[...]
        out = (0.5 * pre * (1.0 + lax.erf(pre * math.sqrt(0.5)))).astype(jnp.bfloat16)
        done = 0
        for at, count in parts:
            feat[at:at + count, :] = out[done:done + count]
            done += count
        totals[...] += jnp.sum(out.astype(jnp.float32).reshape(-1, 8, width), axis=0)

    cuts = list(range(HALO, rows - HALO, STEP)) + [rows - HALO]
    blocks = list(zip(cuts[:-1], cuts[1:]))
    block([(blocks[0][0], blocks[0][1] - blocks[0][0])])
    pl.semaphore_wait(barrier, signals)
    send_up = pltpu.make_async_remote_copy(
        src_ref=x_hbm.at[0, pl.ds(rows - HALO, HALO)], dst_ref=xb.at[pl.ds(0, HALO)],
        send_sem=halo_sem.at[0], recv_sem=halo_sem.at[1], device_id={"frame": up}, device_id_type=pl.DeviceIdType.MESH)
    send_down = pltpu.make_async_remote_copy(
        src_ref=x_hbm.at[0, pl.ds(0, HALO)], dst_ref=xb.at[pl.ds(rows + HALO, HALO)],
        send_sem=halo_sem.at[2], recv_sem=halo_sem.at[3], device_id={"frame": down}, device_id_type=pl.DeviceIdType.MESH)
    send_up.start()
    send_down.start()
    for lo, hi in blocks[1:]:
        block([(lo, hi - lo)])
    send_up.wait()
    send_down.wait()
    widen(0, HALO)
    widen(rows + HALO, HALO)
    block([(0, HALO), (rows - HALO, HALO)])
    save = pltpu.make_async_copy(feat, feat_hbm.at[0], in_sem.at[3])
    save.start()
    n, m = width // TILE, lab.shape[1] // TILE
    units = TILE // 8

    def tdot(p, q):
        return lax.dot_general(p, q, (((0,), (0,)), ((), ())), preferred_element_type=jnp.float32)

    def put(ref, slot, tile):
        ref[slot * units:(slot + 1) * units] = tile.reshape(units, 8, TILE)

    streams = [
        Stream(plan, src, out, *boxes[3 * i:3 * i + 3])
        for i, (plan, src, out) in enumerate(zip(plans, (a_src, b_src, x_src), (a_out, b_out, x_out)))
    ]
    load_l.wait()
    ft = jnp.sum(totals[...], axis=0, keepdims=True)
    lt = jnp.sum(lab[...], axis=0, keepdims=True).astype(jnp.float32)
    hold = TILE // 2
    sums = [v[:, c:c + hold] for v in (ft, lt) for c in range(0, v.shape[1], hold)]
    line = tdot(feat[:, :TILE], feat[...])
    corner = jnp.concatenate(sums + [jnp.zeros((hold - len(sums), hold), jnp.float32)], axis=0)
    head = line[:, :TILE]
    head = jnp.concatenate([head[:hold], jnp.concatenate([corner, head[hold:, hold:]], axis=1)], axis=0)
    put(a_src, 0, head)
    for j in range(1, n):
        put(a_src, j, line[:, j * TILE:(j + 1) * TILE])
    if a_src.shape[0] > n * units:
        a_src[n * units:] = jnp.zeros((a_src.shape[0] - n * units, 8, TILE), jnp.float32)
    streams[0].start()
    slot = 0
    for i in range(1, n):
        line = tdot(feat[:, i * TILE:(i + 1) * TILE], feat[:, i * TILE:])
        for j in range(n - i):
            put(b_src, slot, line[:, j * TILE:(j + 1) * TILE])
            slot += 1
    if b_src.shape[0] > slot * units:
        b_src[slot * units:] = jnp.zeros((b_src.shape[0] - slot * units, 8, TILE), jnp.float32)
    streams[1].start()
    cross = tdot(feat[...], lab[...].astype(jnp.float32).astype(jnp.bfloat16))
    for i in range(n):
        for j in range(m):
            put(x_src, i * m + j, cross[i * TILE:(i + 1) * TILE, j * TILE:(j + 1) * TILE])
    if x_src.shape[0] > n * m * units:
        x_src[n * m * units:] = jnp.zeros((x_src.shape[0] - n * m * units, 8, TILE), jnp.float32)
    streams[2].start()
    gram0, gram1, cross_sums = streams

    def step(stream):
        stream.finish()
        if not stream.done():
            stream.start()

    for stream in (gram0, gram1, cross_sums, gram0, gram1, gram0, cross_sums):
        step(stream)
    while not gram0.done():
        step(gram0)
    centre = Centre(float(rows * sizes[0] * sizes[1]), n, m, tile_at(a_out, 0))
    centre.gram(a_ref, 0, 0, centre.mirror(tile_at(a_out, 0)))
    for j in range(1, n):
        centre.gram(a_ref, 0, j, tile_at(a_out, j))
    for k in range(n):
        invert_block(a_ref, inv_ref, k)
        if k == 0:
            step(gram1)
            step(cross_sums)
        if k < n - 1:
            scale_row(a_ref, inv_ref, w_ref, k)
            if k == 0:
                while not gram1.done():
                    step(gram1)
                for i, j in pairs(n)[n:]:
                    centre.gram(a_ref, i, j, tile_at(b_out, pairs(n).index((i, j)) - n))
            update_rest(a_ref, w_ref, k)
        if k and not cross_sums.done():
            step(cross_sums)
    while not cross_sums.done():
        step(cross_sums)
    for i in range(n):
        for j in range(m):
            centre.cross(c_ref, i, j, tile_at(x_out, i * m + j))
    sent = []

    def ready(k):
        at = pl.ds(k * TILE, TILE)
        copy = pltpu.make_async_copy(y_ref.at[at], y_hbm.at[at], out_sem.at[k])
        copy.start()
        sent.append(copy)

    substitute(inv_ref, w_ref, c_ref, y_ref, ready)
    for copy in sent:
        copy.wait()
    save.wait()


def front(inputs, conv_weight, conv_bias, labels, rec_span):
    sizes = (lax.axis_size("frame"), lax.axis_size("rec"))
    devices = sizes[0] * sizes[1]
    rows, cin = inputs.shape[1:]
    taps, _, width = conv_weight.shape
    wide = labels.shape[2]
    n, m = width // TILE, wide // TILE
    tiles = [n, n * (n - 1) // 2, n * m]
    units = [-(-t * (TILE // 8) // devices) * devices for t in tiles]
    vm = pl.BlockSpec(memory_space=pltpu.VMEM)
    hbm = pl.BlockSpec(memory_space=pltpu.HBM)
    plans = [groups_of(sizes, 4), groups_of(sizes, 4), groups_of(sizes, 2)]
    boxes = [v for plan, u in zip(plans, units) for v in stream_scratch(plan, u)]
    return pl.pallas_call(
        lambda *r: front_kernel(sizes, *r),
        out_shape=[jax.ShapeDtypeStruct((1, rows, width), jnp.bfloat16)]
        + [jax.ShapeDtypeStruct((width, wide), jnp.float32)],
        in_specs=[hbm, hbm, vm, hbm, vm],
        out_specs=[hbm, hbm],
        scratch_shapes=[
            pltpu.VMEM((rows + 2 * HALO, cin), jnp.bfloat16),
            pltpu.VMEM((cin // TILE, rows + 2 * HALO, TILE), jnp.float32),
            pltpu.VMEM(conv_weight.shape, jnp.bfloat16),
            pltpu.VMEM((rows, wide), jnp.int32),
            pltpu.VMEM((2, rows, TILE), jnp.float32),
            pltpu.VMEM((rows, width), jnp.bfloat16),
            pltpu.VMEM((8, width), jnp.float32),
            pltpu.SemaphoreType.DMA((4,)),
            pltpu.SemaphoreType.DMA((4,)),
            pltpu.SemaphoreType.DMA((n,)),
            pltpu.VMEM((width, width), jnp.float32),
            pltpu.VMEM((width, TILE), jnp.float32),
            pltpu.VMEM((width, width), jnp.float32),
            pltpu.VMEM((width, wide), jnp.float32),
            pltpu.VMEM((width, wide), jnp.float32),
        ] + [pltpu.VMEM((u, 8, TILE), jnp.float32) for u in units * 2] + boxes,
        compiler_params=pltpu.CompilerParams(collective_id=0, has_side_effects=True, vmem_limit_bytes=60 << 20),
    )(inputs, conv_weight, conv_bias.reshape(1, width), labels, rec_span)


def per_device(inputs, conv_weight, conv_bias, labels, rec_span):
    features, probe_weights = front(inputs, conv_weight, conv_bias, labels, rec_span)
    return (features, probe_weights)


def solution(mesh):
    in_specs = (P("rec", "frame", None), P(), P(), P("rec", "frame", None), P(None, "rec", "frame"))
    out_specs = (P("rec", "frame", None), P())
    return jax.shard_map(
        per_device, mesh=mesh, in_specs=in_specs, out_specs=out_specs, check_vma=False
    )
```

```python
import math
import jax
import jax.numpy as jnp
from jax import lax
from jax.experimental import pallas as pl
from jax.experimental.pallas import tpu as pltpu
from jax.sharding import PartitionSpec as P

RIDGE = 0.1
TILE = 128
HI = lax.Precision.HIGHEST
GROUP = 16
HALO = 16
STEP = 256

def mm(a, b):
    return jnp.dot(a, b, precision=HI, preferred_element_type=jnp.float32)

def mtm(a, b):
    return lax.dot_general(a, b, (((0,), (0,)), ((), ())), precision=HI, preferred_element_type=jnp.float32)

def spread(row, width):
    return jnp.broadcast_to(row, (8, width))

def tree(terms):
    while len(terms) > 1:
        terms = [terms[i] + terms[i + 1] if i + 1 < len(terms) else terms[i] for i in range(0, len(terms), 2)]
    return terms[0]

def invert_tile(slabs, between):
    count = len(slabs)
    width = 8 * count
    lane = lax.broadcasted_iota(jnp.int32, (8, width), 1)
    sub = lax.broadcasted_iota(jnp.int32, (8, width), 0)
    homes = GROUP // 8
    zero = jnp.zeros((8, width), jnp.float32)
    for j in range(0, width, GROUP):
        first = j // 8
        in_group = (lane >= j) & (lane < j + GROUP)
        near = list(range(first, min(count, first + 2 * homes)))
        cols = {i: [jnp.broadcast_to(slabs[i][:, j + b:j + b + 1], (8, width)) for b in range(GROUP)] for i in near}
        hc = [list(cols[first + t]) for t in range(homes)]
        u = [jnp.where(in_group, jnp.where(lane - sub == j + 8 * t, 1.0, 0.0), slabs[first + t]) for t in range(homes)]
        scale = [jnp.ones((8, width), jnp.float32)] * homes
        for p in range(GROUP):
            h, s = p // 8, p % 8
            r = 1.0 / spread(hc[h][p][s:s + 1], width)
            m = [jnp.where(sub == s, 0.0, hc[t][p]) if t == h else hc[t][p] for t in range(homes)]
            for b in range(p + 1, GROUP):
                f = spread(hc[h][b][s:s + 1], width) * r
                for t in range(homes):
                    hc[t][b] = hc[t][b] - m[t] * f
            row = spread(u[h][s:s + 1], width) * r
            for t in range(homes):
                u[t] = u[t] - m[t] * row
            scale[h] = jnp.where(sub == s, r, scale[h])
        u = [u[t] * scale[t] for t in range(homes)]
        fresh = list(slabs)
        for t in range(homes):
            fresh[first + t] = u[t]
        nxt = near[homes:]
        if nxt:
            rows = [spread(u[b // 8][b % 8:b % 8 + 1], width) for b in range(GROUP)]
            for i in nxt:
                fresh[i] = jnp.where(in_group, 0.0, slabs[i]) - tree([cols[i][b] * rows[b] for b in range(GROUP)])
        left = jnp.concatenate(slabs, axis=0)
        right = jnp.concatenate([u[i - first] if first <= i < first + homes else zero for i in range(count)], axis=0)
        prod = mm(left, right)
        for i in range(count):
            if i not in near:
                fresh[i] = jnp.where(in_group, 0.0, slabs[i]) - prod[8 * i:8 * i + 8]
        slabs = fresh
        between(j // GROUP)
    return slabs

def invert_block(a_ref, inv_ref, k, between):
    lo, hi = k * TILE, (k + 1) * TILE
    slabs = invert_tile([a_ref[lo + 8 * i:lo + 8 * i + 8, lo:hi] for i in range(TILE // 8)], between)
    for i, s in enumerate(slabs):
        inv_ref[lo + 8 * i:lo + 8 * i + 8, :] = s


def scale_row(a_ref, inv_ref, w_ref, k, first, last):
    lo, hi = k * TILE, (k + 1) * TILE
    s = slice(first * TILE, last * TILE)
    w_ref[lo:hi, s] = mm(inv_ref[lo:hi, :], a_ref[lo:hi, s])


def update(a_ref, w_ref, k, i, first, last):
    lo, hi = k * TILE, (k + 1) * TILE
    s = slice(first * TILE, last * TILE)
    rows = slice(i * TILE, (i + 1) * TILE)
    a_ref[rows, s] -= mtm(a_ref[lo:hi, rows], w_ref[lo:hi, s])


def forward(w_ref, c_ref, k):
    lo, hi = k * TILE, (k + 1) * TILE
    c_ref[hi:, :] -= mtm(w_ref[lo:hi, hi:], c_ref[lo:hi, :])


def backward(inv_ref, w_ref, c_ref, y_ref):
    n = y_ref.shape[0] // TILE
    for k in reversed(range(n)):
        lo, hi = k * TILE, (k + 1) * TILE
        y = mm(inv_ref[lo:hi, :], c_ref[lo:hi, :])
        if k < n - 1:
            y = y - mm(w_ref[lo:hi, hi:], y_ref[hi:, :])
        y_ref[lo:hi, :] = y


def swap_halves(v):
    return pltpu.roll(v, TILE // 2, 1)


def bits_of(axis, size):
    return [(axis, 1 << i) for i in range(size.bit_length() - 1)]


def pairs(n):
    return [(i, j) for i in range(n) for j in range(i, n)]


def wanted(n):
    first = [(0, 0), (0, 1), (1, 1), (0, 2)]
    return [first[:2], first[2:], [p for p in pairs(n) if p not in first]]


def groups_of(sizes, most):
    frame, rec = bits_of("frame", sizes[0]), bits_of("rec", sizes[1])
    rest = rec[1:2] + frame[:1] + frame[1:] + rec[2:]
    return [rec[:1]] + [rest[i:i + most] for i in range(0, len(rest), most)]


def bit_values(group):
    return [lax.rem(lax.axis_index(axis) // step, 2) for axis, step in group]


def peer_of(group, bits, mask):
    place = {}
    for i, (axis, step) in enumerate(group):
        if mask >> i & 1:
            place[axis] = place.get(axis, lax.axis_index(axis)) + (1 - 2 * bits[i]) * step
    return place


def rank_of(bits, mask=0):
    return sum((1 - v if mask >> i & 1 else v) * (1 << i) for i, v in enumerate(bits))


def inbox_units(groups, units):
    total = 0
    for group in groups:
        chunk = units >> len(group)
        total += units - chunk
        units = chunk
    return total


def copies_of(groups):
    return 2 * sum((1 << len(g)) - 1 for g in groups)


class Stream:
    def __init__(self, groups, split, src, out, acc, inbox, sems):
        self.phases = 2 * len(groups) - split
        self.groups, self.src, self.out, self.acc, self.inbox, self.sems = groups, src, out, acc, inbox, sems
        self.length, self.lo, self.at = src.shape[0], 0, 0
        self.held, self.used, self.kept, self.sem = (src, 0), 0, 0, 0
        self.copies = []

    def done(self):
        return self.at == self.phases

    def start(self):
        count = len(self.groups)
        self.down = self.at < count
        self.group = self.groups[self.at if self.down else 2 * count - 1 - self.at]
        self.bits = bit_values(self.group)
        self.copies = []
        self.chunk = self.length >> len(self.group)
        for mask in range(1, 1 << len(self.group)):
            if self.down:
                ref, base = self.held
                src = ref.at[pl.ds(base + rank_of(self.bits, mask) * self.chunk, self.chunk)]
                dst = self.inbox.at[pl.ds(self.used + (mask - 1) * self.chunk, self.chunk)]
            else:
                src = dst = self.out.at[pl.ds(self.lo, self.length)]
            copy = pltpu.make_async_remote_copy(
                src_ref=src, dst_ref=dst,
                send_sem=self.sems.at[0, self.sem], recv_sem=self.sems.at[1, self.sem],
                device_id=peer_of(self.group, self.bits, mask), device_id_type=pl.DeviceIdType.MESH,
            )
            copy.start()
            self.copies.append(copy)
            self.sem += 1

    def finish(self):
        for copy in self.copies:
            copy.wait()
        rank = rank_of(self.bits)
        if self.down:
            ref, base = self.held
            total = ref[pl.ds(base + rank * self.chunk, self.chunk)]
            for i in range((1 << len(self.group)) - 1):
                total = total + self.inbox[self.used + i * self.chunk:self.used + (i + 1) * self.chunk]
            self.used += self.length - self.chunk
            self.lo, self.length = self.lo + rank * self.chunk, self.chunk
            if self.at < len(self.groups) - 1:
                self.acc[self.kept:self.kept + self.chunk] = total
                self.held = (self.acc, self.kept)
                self.kept += self.chunk
            else:
                self.out[pl.ds(self.lo, self.chunk)] = total
        else:
            self.lo = self.lo - rank * self.length
            self.length = self.length << len(self.group)
        self.at += 1


def stream_scratch(groups, units):
    held = sum(units >> sum(len(g) for g in groups[:i + 1]) for i in range(len(groups) - 1))
    return [
        pltpu.VMEM((max(held, 1), 8, TILE), jnp.float32),
        pltpu.VMEM((inbox_units(groups, units), 8, TILE), jnp.float32),
        pltpu.SemaphoreType.DMA((2, copies_of(groups))),
    ]


def greet(plans, size):
    barrier = pltpu.get_barrier_semaphore()
    met = {}
    for groups in plans:
        for group in groups:
            for mask in range(1, 1 << len(group)):
                met[tuple(sorted(bit for i, bit in enumerate(group) if mask >> i & 1))] = (group, mask)
    for group, mask in met.values():
        pl.semaphore_signal(barrier, inc=1, device_id=peer_of(group, bit_values(group), mask), device_id_type=pl.DeviceIdType.MESH)
    me = lax.axis_index("frame")
    for there, peer in ((me < size - 1, me + 1), (me > 0, me - 1)):
        @pl.when(there)
        def _():
            pl.semaphore_signal(barrier, inc=1, device_id={"frame": peer}, device_id_type=pl.DeviceIdType.MESH)
    return barrier, len(met) + 2 - jnp.where(me == 0, 1, 0) - jnp.where(me == size - 1, 1, 0)


def tile_at(ref, slot):
    units = TILE // 8
    return ref[slot * units:(slot + 1) * units].reshape(TILE, TILE)


def column(totals, i):
    return jnp.broadcast_to(totals[i:i + 1], (TILE, TILE)).T


class Centre:
    def __init__(self, frames, n, m, head):
        hold = TILE // 2
        sums = head[hold:, :hold]
        self.frames, self.n = frames, n
        self.totals = jnp.concatenate(
            [jnp.concatenate([sums[2 * i:2 * i + 1], sums[2 * i + 1:2 * i + 2]], axis=1) for i in range(n + m)], axis=0)
        self.cols = [column(self.totals, i) for i in range(n)]
        self.down = lax.broadcasted_iota(jnp.int32, (TILE, TILE), 0)
        self.across = lax.broadcasted_iota(jnp.int32, (TILE, TILE), 1)

    def mirror(self, tile):
        return jnp.where(self.down <= self.across, tile, tile.T)

    def gram(self, a_ref, i, j, tile):
        v = (tile - self.cols[i] * self.totals[j:j + 1] / self.frames) / self.frames
        if i == j:
            v = v + jnp.where(self.down == self.across, RIDGE, 0.0)
        a_ref[i * TILE:(i + 1) * TILE, j * TILE:(j + 1) * TILE] = v

    def cross(self, c_ref, block, own, packed):
        labels = jnp.zeros((1, TILE), jnp.float32)
        for q in range(2 * (self.totals.shape[0] - self.n)):
            line = self.totals[self.n + q // 2:self.n + q // 2 + 1]
            labels = jnp.where(block == q, swap_halves(line) if q % 2 else line, labels)
        packed = jnp.where(own == 1, swap_halves(packed), packed)
        rows = packed.shape[0]
        for at, part in ((0, packed), (rows, swap_halves(packed))):
            for i in range(rows // TILE):
                lo = at + i * TILE
                v = part[i * TILE:(i + 1) * TILE] - self.cols[lo // TILE] * labels / self.frames
                c_ref[lo:lo + TILE, :] = v / math.sqrt(self.frames)


def front_kernel(sizes, x_hbm, w_hbm, bias_ref, lab_hbm, span_ref, feat_hbm, y_hbm,
                 xb, xf, w, lab, mask, feat, totals, in_sem, halo_sem, out_sem, a_ref, inv_ref, w_ref, c_ref, y_ref,
                 z_ref, z_sem, out_ref, *boxes):
    rows, cin = x_hbm.shape[1], x_hbm.shape[2]
    taps, width = w_hbm.shape[0], w_hbm.shape[2]
    half = taps // 2
    chunks = cin // TILE
    size = sizes[0]
    me = lax.axis_index("frame")
    up, down = me + 1, me - 1
    has_up, has_down = me < size - 1, me > 0
    plans = [groups_of(sizes, 4)] * 3 + [groups_of(sizes, 2)]
    barrier, signals = greet(plans, size)
    load_x = pltpu.make_async_copy(x_hbm.at[0], xb.at[pl.ds(HALO, rows)], in_sem.at[0])
    load_x.start()
    load_w = pltpu.make_async_copy(w_hbm, w, in_sem.at[1])
    load_w.start()
    load_l = pltpu.make_async_copy(lab_hbm.at[0], lab, in_sem.at[2])
    load_l.start()
    for i in range(rows // TILE):
        for side in range(2):
            line = span_ref[side, 0:1, i * TILE:(i + 1) * TILE].astype(jnp.float32)
            mask[side, i * TILE:(i + 1) * TILE, :] = jnp.broadcast_to(line, (TILE, TILE)).T
    load_x.wait()

    def widen(lo, count):
        for c in range(chunks):
            xf[c, lo:lo + count, :] = xb[lo:lo + count, c * TILE:(c + 1) * TILE].astype(jnp.float32)
    widen(HALO, rows)
    load_w.wait()
    totals[...] = jnp.zeros_like(totals)

    def taps_at(at, count):
        pieces = []
        for k in range(taps):
            off = k - half
            base = HALO + at
            if off == 0:
                pieces.append(xb[base:base + count, :])
                continue
            keep = mask[0 if off < 0 else 1, at:at + count, :] >= abs(off)
            for c in range(chunks):
                v = xf[c, base + off:base + off + count, :]
                pieces.append(jnp.where(keep, v, 0.0).astype(jnp.bfloat16))
        return jnp.concatenate(pieces, axis=1)

    def block(parts):
        stacked = [taps_at(at, count) for at, count in parts]
        stacked = stacked[0] if len(stacked) == 1 else jnp.concatenate(stacked, axis=0)
        pre = jnp.dot(stacked, w[...].reshape(taps * cin, width), preferred_element_type=jnp.float32) + bias_ref[...]
        out = (0.5 * pre * (1.0 + lax.erf(pre * math.sqrt(0.5)))).astype(jnp.bfloat16)
        done = 0
        for at, count in parts:
            feat[at:at + count, :] = out[done:done + count]
            done += count
        totals[...] += jnp.sum(out.astype(jnp.float32).reshape(-1, 8, width), axis=0)

    cuts = list(range(HALO, rows - HALO, STEP)) + [rows - HALO]
    blocks = list(zip(cuts[:-1], cuts[1:]))
    block([(blocks[0][0], blocks[0][1] - blocks[0][0])])
    pl.semaphore_wait(barrier, signals)
    send_up = pltpu.make_async_remote_copy(
        src_ref=x_hbm.at[0, pl.ds(rows - HALO, HALO)], dst_ref=xb.at[pl.ds(0, HALO)],
        send_sem=halo_sem.at[0], recv_sem=halo_sem.at[1], device_id={"frame": up}, device_id_type=pl.DeviceIdType.MESH)
    send_down = pltpu.make_async_remote_copy(
        src_ref=x_hbm.at[0, pl.ds(0, HALO)], dst_ref=xb.at[pl.ds(rows + HALO, HALO)],
        send_sem=halo_sem.at[2], recv_sem=halo_sem.at[3], device_id={"frame": down}, device_id_type=pl.DeviceIdType.MESH)

    @pl.when(has_up)
    def _():
        send_up.start()

    @pl.when(has_down)
    def _():
        send_down.start()

    @pl.when(jnp.logical_not(has_down))
    def _():
        xb[:HALO, :] = jnp.zeros((HALO, cin), jnp.bfloat16)

    @pl.when(jnp.logical_not(has_up))
    def _():
        xb[rows + HALO:, :] = jnp.zeros((HALO, cin), jnp.bfloat16)

    for lo, hi in blocks[1:]:
        block([(lo, hi - lo)])

    @pl.when(has_up)
    def _():
        send_up.wait_send()
        send_down.wait_recv()

    @pl.when(has_down)
    def _():
        send_down.wait_send()
        send_up.wait_recv()

    widen(0, HALO)
    widen(rows + HALO, HALO)
    block([(0, HALO), (rows - HALO, HALO)])
    save = pltpu.make_async_copy(feat, feat_hbm.at[0], in_sem.at[3])
    save.start()
    n, m = width // TILE, lab.shape[1] // TILE
    units = TILE // 8

    def tdot(p, q):
        return lax.dot_general(p, q, (((0,), (0,)), ((), ())), preferred_element_type=jnp.float32)

    def put(ref, slot, tile):
        ref[slot * units:(slot + 1) * units] = tile.reshape(units, 8, TILE)

    streams = [
        Stream(plan, 2 * (i == len(plans) - 1), boxes[i], boxes[len(plans) + i], *boxes[2 * len(plans) + 3 * i:2 * len(plans) + 3 * i + 3])
        for i, plan in enumerate(plans)
    ]
    load_l.wait()
    ft = jnp.sum(totals[...], axis=0, keepdims=True)
    lt = jnp.sum(lab[...], axis=0, keepdims=True).astype(jnp.float32)
    hold = TILE // 2
    sums = [v[:, c:c + hold] for v in (ft, lt) for c in range(0, v.shape[1], hold)]
    corner = jnp.concatenate(sums + [jnp.zeros((hold - len(sums), hold), jnp.float32)], axis=0)
    for stream, some in zip(streams, wanted(n)):
        src = stream.src
        at = 0
        while at < len(some):
            i, j = some[at]
            run = 1
            while at + run < len(some) and some[at + run] == (i, j + run):
                run += 1
            line = tdot(feat[:, i * TILE:(i + 1) * TILE], feat[:, j * TILE:(j + run) * TILE])
            for r in range(run):
                tile = line[:, r * TILE:(r + 1) * TILE]
                if (i, j + r) == (0, 0):
                    tile = jnp.concatenate([tile[:hold], jnp.concatenate([corner, tile[hold:, hold:]], axis=1)], axis=0)
                put(src, at + r, tile)
            at += run
        if src.shape[0] > len(some) * units:
            src[len(some) * units:] = jnp.zeros((src.shape[0] - len(some) * units, 8, TILE), jnp.float32)
        stream.start()
    x_src = streams[-1].src
    left = lax.broadcasted_iota(jnp.int32, (width // 2, TILE), 1) < TILE // 2
    for j in range(m):
        flags = lab[:, j * TILE:(j + 1) * TILE].astype(jnp.float32).astype(jnp.bfloat16)
        line = tdot(feat[...], flags)
        top, low = line[:width // 2], swap_halves(line[width // 2:])
        for q, v in ((2 * j, jnp.where(left, top, low)), (2 * j + 1, jnp.where(left, low, top))):
            x_src[q * width // 16:(q + 1) * width // 16] = v.reshape(width // 16, 8, TILE)
    streams[-1].start()
    gram0, gram1, gram2, cross_sums = streams

    def step(*some):
        for stream in some:
            if not stream.done():
                stream.finish()
                if not stream.done():
                    stream.start()

    def drain(stream):
        while not stream.done():
            step(stream)

    spread_bits = [bit_values(group) for group in plans[-1][:2]]
    ranks = [rank_of(bits) for bits in spread_bits]
    block = (ranks[0] << len(spread_bits[1])) + ranks[1]
    odd = lax.rem(block, 2)
    polls = {(0, 2): [gram1], (0, 5): [gram2], (0, 6): [cross_sums], (1, 6): [cross_sums]}

    def invert(k):
        invert_block(a_ref, inv_ref, k, lambda g: step(*polls.get((k, g), [])))

    def centre_tiles(which):
        for slot, (i, j) in enumerate(wanted(n)[which]):
            tile = tile_at(streams[which].out, slot)
            centre.gram(a_ref, i, j, centre.mirror(tile) if (i, j) == (0, 0) else tile)

    step(gram0, gram1, gram2)
    step(gram0, gram1, cross_sums, gram2)
    drain(gram0)
    centre = Centre(float(rows * sizes[0] * sizes[1]), n, m, tile_at(gram0.out, 0))
    centre_tiles(0)
    invert(0)
    scale_row(a_ref, inv_ref, w_ref, 0, 1, 2)
    drain(gram1)
    centre_tiles(1)
    update(a_ref, w_ref, 0, 1, 1, 2)
    invert(1)
    drain(gram2)
    centre_tiles(2)
    scale_row(a_ref, inv_ref, w_ref, 0, 2, n)
    for i in range(1, n):
        update(a_ref, w_ref, 0, i, max(i, 2), n)
    for k in range(1, n):
        if k > 1:
            invert(k)
        if k < n - 1:
            scale_row(a_ref, inv_ref, w_ref, k, k + 1, n)
            for i in range(k + 1, n):
                update(a_ref, w_ref, k, i, i, n)
        if k == n - 2:
            drain(cross_sums)
            packed = cross_sums.out[pl.ds(block * (width // 16), width // 16)].reshape(width // 2, TILE)
            centre.cross(c_ref, block, odd, packed)
            for i in range(n - 1):
                forward(w_ref, c_ref, i)
    backward(inv_ref, w_ref, c_ref, y_ref)
    packed = jnp.where(left, y_ref[:width // 2, :], swap_halves(y_ref[width // 2:, :]))
    packed = jnp.where(odd == 1, swap_halves(packed), packed)
    share = width // 2
    z_ref[pl.ds(pl.multiple_of(block * share, share), share), :] = packed.astype(jnp.bfloat16)
    held, used = 1, 0
    for group, bits in ((plans[-1][1], spread_bits[1]), (plans[-1][0], spread_bits[0])):
        first = block if held == 1 else ranks[0] * held
        span = pl.ds(pl.multiple_of(first * share, share), held * share)
        copies = []
        for other in range(1, 1 << len(group)):
            copy = pltpu.make_async_remote_copy(
                src_ref=z_ref.at[span], dst_ref=z_ref.at[span],
                send_sem=z_sem.at[0, used], recv_sem=z_sem.at[1, used],
                device_id=peer_of(group, bits, other), device_id_type=pl.DeviceIdType.MESH,
            )
            copy.start()
            copies.append(copy)
            used += 1
        for copy in copies:
            copy.wait()
        held <<= len(group)
    for j in range(m):
        even, uneven = [z_ref[q * share:(q + 1) * share, :].astype(jnp.float32) for q in (2 * j, 2 * j + 1)]
        out_ref[:share, j * TILE:(j + 1) * TILE] = jnp.where(left, even, uneven).astype(jnp.bfloat16)
        out_ref[share:, j * TILE:(j + 1) * TILE] = swap_halves(jnp.where(left, uneven, even)).astype(jnp.bfloat16)
    leave = pltpu.make_async_copy(out_ref, y_hbm, out_sem.at[0])
    leave.start()
    leave.wait()
    save.wait()


def front(inputs, conv_weight, conv_bias, labels, rec_span):
    sizes = (lax.axis_size("frame"), lax.axis_size("rec"))
    devices = sizes[0] * sizes[1]
    rows, cin = inputs.shape[1:]
    taps, _, width = conv_weight.shape
    wide = labels.shape[2]
    n, m = width // TILE, wide // TILE
    tiles = [len(some) for some in wanted(n)] + [n * m]
    units = [-(-t * (TILE // 8) // devices) * devices for t in tiles]
    vm = pl.BlockSpec(memory_space=pltpu.VMEM)
    hbm = pl.BlockSpec(memory_space=pltpu.HBM)
    plans = [groups_of(sizes, 4)] * 3 + [groups_of(sizes, 2)]
    boxes = [v for plan, u in zip(plans, units) for v in stream_scratch(plan, u)]
    return pl.pallas_call(
        lambda *r: front_kernel(sizes, *r),
        out_shape=[jax.ShapeDtypeStruct((1, rows, width), jnp.bfloat16)]
        + [jax.ShapeDtypeStruct((width, wide), jnp.bfloat16)],
        in_specs=[hbm, hbm, vm, hbm, vm],
        out_specs=[hbm, hbm],
        scratch_shapes=[
            pltpu.VMEM((rows + 2 * HALO, cin), jnp.bfloat16),
            pltpu.VMEM((cin // TILE, rows + 2 * HALO, TILE), jnp.float32),
            pltpu.VMEM(conv_weight.shape, jnp.bfloat16),
            pltpu.VMEM((rows, wide), jnp.int32),
            pltpu.VMEM((2, rows, TILE), jnp.float32),
            pltpu.VMEM((rows, width), jnp.bfloat16),
            pltpu.VMEM((8, width), jnp.float32),
            pltpu.SemaphoreType.DMA((4,)),
            pltpu.SemaphoreType.DMA((4,)),
            pltpu.SemaphoreType.DMA((n,)),
            pltpu.VMEM((width, width), jnp.float32),
            pltpu.VMEM((width, TILE), jnp.float32),
            pltpu.VMEM((width, width), jnp.float32),
            pltpu.VMEM((width, TILE), jnp.float32),
            pltpu.VMEM((width, TILE), jnp.float32),
            pltpu.VMEM((wide * width // TILE, TILE), jnp.bfloat16),
            pltpu.SemaphoreType.DMA((2, copies_of(plans[-1][:2]) // 2)),
            pltpu.VMEM((width, wide), jnp.bfloat16),
        ] + [pltpu.VMEM((u, 8, TILE), jnp.float32) for u in units * 2] + boxes,
        compiler_params=pltpu.CompilerParams(collective_id=0, has_side_effects=True, vmem_limit_bytes=60 << 20),
    )(inputs, conv_weight, conv_bias.reshape(1, width), labels, rec_span)


def leave_kernel(feat_in, y_in, feat_out, y_out, feat, held, wide, sems):
    count = sems.shape[1] // 2
    fetch, store = [], []
    rows, lines = y_in.shape[0] // count, feat_in.shape[1] // count
    for i in range(count):
        p = pl.ds(i * rows, rows)
        fetch.append(pltpu.make_async_copy(y_in.at[p], held.at[p], sems.at[0, i]))
        store.append(pltpu.make_async_copy(wide.at[p], y_out.at[p], sems.at[1, i]))
    for i in range(count):
        p = pl.ds(i * lines, lines)
        fetch.append(pltpu.make_async_copy(feat_in.at[0, p], feat.at[p], sems.at[0, count + i]))
        store.append(pltpu.make_async_copy(feat.at[p], feat_out.at[0, p], sems.at[1, count + i]))
    for copy in fetch:
        copy.start()
    for i in range(2 * count):
        fetch[i].wait()
        if i < count:
            wide[i * rows:(i + 1) * rows, :] = held[i * rows:(i + 1) * rows, :].astype(jnp.float32)
        store[i].start()
    for copy in store:
        copy.wait()


def leave(features, y):
    hbm = pl.BlockSpec(memory_space=pltpu.HBM)
    return pl.pallas_call(
        leave_kernel,
        out_shape=[jax.ShapeDtypeStruct(features.shape, features.dtype), jax.ShapeDtypeStruct(y.shape, jnp.float32)],
        in_specs=[hbm, hbm],
        out_specs=[hbm, hbm],
        scratch_shapes=[
            pltpu.VMEM(features.shape[1:], features.dtype),
            pltpu.VMEM(y.shape, y.dtype),
            pltpu.VMEM(y.shape, jnp.float32),
            pltpu.SemaphoreType.DMA((2, 4)),
        ],
        compiler_params=pltpu.CompilerParams(vmem_limit_bytes=60 << 20),
    )(features, y)


def per_device(inputs, conv_weight, conv_bias, labels, rec_span):
    features, probe_weights = front(inputs, conv_weight, conv_bias, labels, rec_span)
    return tuple(leave(features, probe_weights))


def solution(mesh):
    in_specs = (P("rec", "frame", None), P(), P(), P("rec", "frame", None), P(None, "rec", "frame"))
    out_specs = (P("rec", "frame", None), P())
    return jax.shard_map(
        per_device, mesh=mesh, in_specs=in_specs, out_specs=out_specs, check_vma=False
    )
```

```python
import math
import jax
import jax.numpy as jnp
from jax import lax
from jax.experimental import pallas as pl
from jax.experimental.pallas import tpu as pltpu
from jax.sharding import PartitionSpec as P

RIDGE = 0.1
TILE = 128
HI = lax.Precision.HIGHEST
GROUP = 16
HALO = 16
STEP = 256

def mm(a, b):
    return jnp.dot(a, b, precision=HI, preferred_element_type=jnp.float32)

def mtm(a, b):
    return lax.dot_general(a, b, (((0,), (0,)), ((), ())), precision=HI, preferred_element_type=jnp.float32)

def spread(row, width):
    return jnp.broadcast_to(row, (8, width))

def tree(terms):
    while len(terms) > 1:
        terms = [terms[i] + terms[i + 1] if i + 1 < len(terms) else terms[i] for i in range(0, len(terms), 2)]
    return terms[0]

def invert_tile(slabs, between):
    count = len(slabs)
    width = 8 * count
    lane = lax.broadcasted_iota(jnp.int32, (8, width), 1)
    sub = lax.broadcasted_iota(jnp.int32, (8, width), 0)
    homes = GROUP // 8
    zero = jnp.zeros((8, width), jnp.float32)
    for j in range(0, width, GROUP):
        first = j // 8
        in_group = (lane >= j) & (lane < j + GROUP)
        near = list(range(first, min(count, first + 2 * homes)))
        cols = {i: [jnp.broadcast_to(slabs[i][:, j + b:j + b + 1], (8, width)) for b in range(GROUP)] for i in near}
        hc = [list(cols[first + t]) for t in range(homes)]
        u = [jnp.where(in_group, jnp.where(lane - sub == j + 8 * t, 1.0, 0.0), slabs[first + t]) for t in range(homes)]
        scale = [jnp.ones((8, width), jnp.float32)] * homes
        for p in range(GROUP):
            h, s = p // 8, p % 8
            r = 1.0 / spread(hc[h][p][s:s + 1], width)
            m = [jnp.where(sub == s, 0.0, hc[t][p]) if t == h else hc[t][p] for t in range(homes)]
            for b in range(p + 1, GROUP):
                f = spread(hc[h][b][s:s + 1], width) * r
                for t in range(homes):
                    hc[t][b] = hc[t][b] - m[t] * f
            row = spread(u[h][s:s + 1], width) * r
            for t in range(homes):
                u[t] = u[t] - m[t] * row
            scale[h] = jnp.where(sub == s, r, scale[h])
        u = [u[t] * scale[t] for t in range(homes)]
        fresh = list(slabs)
        for t in range(homes):
            fresh[first + t] = u[t]
        nxt = near[homes:]
        if nxt:
            rows = [spread(u[b // 8][b % 8:b % 8 + 1], width) for b in range(GROUP)]
            for i in nxt:
                fresh[i] = jnp.where(in_group, 0.0, slabs[i]) - tree([cols[i][b] * rows[b] for b in range(GROUP)])
        left = jnp.concatenate(slabs, axis=0)
        right = jnp.concatenate([u[i - first] if first <= i < first + homes else zero for i in range(count)], axis=0)
        prod = mm(left, right)
        for i in range(count):
            if i not in near:
                fresh[i] = jnp.where(in_group, 0.0, slabs[i]) - prod[8 * i:8 * i + 8]
        slabs = fresh
        between(j // GROUP)
    return slabs

def invert_block(a_ref, inv_ref, k, between):
    lo, hi = k * TILE, (k + 1) * TILE
    slabs = invert_tile([a_ref[lo + 8 * i:lo + 8 * i + 8, lo:hi] for i in range(TILE // 8)], between)
    for i, s in enumerate(slabs):
        inv_ref[lo + 8 * i:lo + 8 * i + 8, :] = s


def scale_row(a_ref, inv_ref, w_ref, k, first, last):
    lo, hi = k * TILE, (k + 1) * TILE
    s = slice(first * TILE, last * TILE)
    w_ref[lo:hi, s] = mm(inv_ref[lo:hi, :], a_ref[lo:hi, s])


def update(a_ref, w_ref, k, i, first, last):
    lo, hi = k * TILE, (k + 1) * TILE
    s = slice(first * TILE, last * TILE)
    rows = slice(i * TILE, (i + 1) * TILE)
    a_ref[rows, s] -= mtm(a_ref[lo:hi, rows], w_ref[lo:hi, s])


def forward(w_ref, c_ref, k):
    lo, hi = k * TILE, (k + 1) * TILE
    c_ref[hi:, :] -= mtm(w_ref[lo:hi, hi:], c_ref[lo:hi, :])


def backward(inv_ref, w_ref, c_ref, y_ref, ready):
    n = y_ref.shape[0] // TILE
    for k in reversed(range(n)):
        lo, hi = k * TILE, (k + 1) * TILE
        y = mm(inv_ref[lo:hi, :], c_ref[lo:hi, :])
        if k < n - 1:
            y = y - mm(w_ref[lo:hi, hi:], y_ref[hi:, :])
        y_ref[lo:hi, :] = y
        ready(k)


def swap_halves(v):
    return pltpu.roll(v, TILE // 2, 1)


def bits_of(axis, size):
    return [(axis, 1 << i) for i in range(size.bit_length() - 1)]


def pairs(n):
    return [(i, j) for i in range(n) for j in range(i, n)]


def wanted(n):
    first = [(0, 0), (0, 1), (1, 1), (0, 2)]
    return [first[:2], first[2:], [p for p in pairs(n) if p not in first]]


def groups_of(sizes, most):
    frame, rec = bits_of("frame", sizes[0]), bits_of("rec", sizes[1])
    rest = rec[1:2] + frame[:1] + frame[1:] + rec[2:]
    return [rec[:1]] + [rest[i:i + most] for i in range(0, len(rest), most)]


def bit_values(group):
    return [lax.rem(lax.axis_index(axis) // step, 2) for axis, step in group]


def peer_of(group, bits, mask):
    place = {}
    for i, (axis, step) in enumerate(group):
        if mask >> i & 1:
            place[axis] = place.get(axis, lax.axis_index(axis)) + (1 - 2 * bits[i]) * step
    return place


def rank_of(bits, mask=0):
    return sum((1 - v if mask >> i & 1 else v) * (1 << i) for i, v in enumerate(bits))


def inbox_units(groups, units):
    total = 0
    for group in groups:
        chunk = units >> len(group)
        total += units - chunk
        units = chunk
    return total


def copies_of(groups):
    return 2 * sum((1 << len(g)) - 1 for g in groups)


class Stream:
    def __init__(self, groups, split, src, out, acc, inbox, sems):
        self.phases = 2 * len(groups) - split
        self.groups, self.src, self.out, self.acc, self.inbox, self.sems = groups, src, out, acc, inbox, sems
        self.length, self.lo, self.at = src.shape[0], 0, 0
        self.held, self.used, self.kept, self.sem = (src, 0), 0, 0, 0
        self.copies = []

    def done(self):
        return self.at == self.phases

    def start(self):
        count = len(self.groups)
        self.down = self.at < count
        self.group = self.groups[self.at if self.down else 2 * count - 1 - self.at]
        self.bits = bit_values(self.group)
        self.copies = []
        self.chunk = self.length >> len(self.group)
        for mask in range(1, 1 << len(self.group)):
            if self.down:
                ref, base = self.held
                src = ref.at[pl.ds(base + rank_of(self.bits, mask) * self.chunk, self.chunk)]
                dst = self.inbox.at[pl.ds(self.used + (mask - 1) * self.chunk, self.chunk)]
            else:
                src = dst = self.out.at[pl.ds(self.lo, self.length)]
            copy = pltpu.make_async_remote_copy(
                src_ref=src, dst_ref=dst,
                send_sem=self.sems.at[0, self.sem], recv_sem=self.sems.at[1, self.sem],
                device_id=peer_of(self.group, self.bits, mask), device_id_type=pl.DeviceIdType.MESH,
            )
            copy.start()
            self.copies.append(copy)
            self.sem += 1

    def finish(self):
        for copy in self.copies:
            copy.wait()
        rank = rank_of(self.bits)
        if self.down:
            ref, base = self.held
            total = ref[pl.ds(base + rank * self.chunk, self.chunk)]
            for i in range((1 << len(self.group)) - 1):
                total = total + self.inbox[self.used + i * self.chunk:self.used + (i + 1) * self.chunk]
            self.used += self.length - self.chunk
            self.lo, self.length = self.lo + rank * self.chunk, self.chunk
            if self.at < len(self.groups) - 1:
                self.acc[self.kept:self.kept + self.chunk] = total
                self.held = (self.acc, self.kept)
                self.kept += self.chunk
            else:
                self.out[pl.ds(self.lo, self.chunk)] = total
        else:
            self.lo = self.lo - rank * self.length
            self.length = self.length << len(self.group)
        self.at += 1


def stream_scratch(groups, units):
    held = sum(units >> sum(len(g) for g in groups[:i + 1]) for i in range(len(groups) - 1))
    return [
        pltpu.VMEM((max(held, 1), 8, TILE), jnp.float32),
        pltpu.VMEM((inbox_units(groups, units), 8, TILE), jnp.float32),
        pltpu.SemaphoreType.DMA((2, copies_of(groups))),
    ]


def greet(plans, size):
    barrier = pltpu.get_barrier_semaphore()
    met = {}
    for groups in plans:
        for group in groups:
            for mask in range(1, 1 << len(group)):
                met[tuple(sorted(bit for i, bit in enumerate(group) if mask >> i & 1))] = (group, mask)
    for group, mask in met.values():
        pl.semaphore_signal(barrier, inc=1, device_id=peer_of(group, bit_values(group), mask), device_id_type=pl.DeviceIdType.MESH)
    me = lax.axis_index("frame")
    for there, peer in ((me < size - 1, me + 1), (me > 0, me - 1)):
        @pl.when(there)
        def _():
            pl.semaphore_signal(barrier, inc=1, device_id={"frame": peer}, device_id_type=pl.DeviceIdType.MESH)
    return barrier, len(met) + 2 - jnp.where(me == 0, 1, 0) - jnp.where(me == size - 1, 1, 0)


def tile_at(ref, slot):
    units = TILE // 8
    return ref[slot * units:(slot + 1) * units].reshape(TILE, TILE)


def column(totals, i):
    return jnp.broadcast_to(totals[i:i + 1], (TILE, TILE)).T


class Centre:
    def __init__(self, frames, n, m, head):
        hold = TILE // 2
        sums = head[hold:, :hold]
        self.frames, self.n = frames, n
        self.totals = jnp.concatenate(
            [jnp.concatenate([sums[2 * i:2 * i + 1], sums[2 * i + 1:2 * i + 2]], axis=1) for i in range(n + m)], axis=0)
        self.cols = [column(self.totals, i) for i in range(n)]
        self.down = lax.broadcasted_iota(jnp.int32, (TILE, TILE), 0)
        self.across = lax.broadcasted_iota(jnp.int32, (TILE, TILE), 1)

    def mirror(self, tile):
        return jnp.where(self.down <= self.across, tile, tile.T)

    def gram(self, a_ref, i, j, tile):
        v = (tile - self.cols[i] * self.totals[j:j + 1] / self.frames) / self.frames
        if i == j:
            v = v + jnp.where(self.down == self.across, RIDGE, 0.0)
        a_ref[i * TILE:(i + 1) * TILE, j * TILE:(j + 1) * TILE] = v

    def cross(self, c_ref, block, own, packed):
        labels = jnp.zeros((1, TILE), jnp.float32)
        for q in range(2 * (self.totals.shape[0] - self.n)):
            line = self.totals[self.n + q // 2:self.n + q // 2 + 1]
            labels = jnp.where(block == q, swap_halves(line) if q % 2 else line, labels)
        packed = jnp.where(own == 1, swap_halves(packed), packed)
        rows = packed.shape[0]
        for at, part in ((0, packed), (rows, swap_halves(packed))):
            for i in range(rows // TILE):
                lo = at + i * TILE
                v = part[i * TILE:(i + 1) * TILE] - self.cols[lo // TILE] * labels / self.frames
                c_ref[lo:lo + TILE, :] = v / math.sqrt(self.frames)


def front_kernel(sizes, x_hbm, w_hbm, bias_ref, lab_hbm, span_ref, feat_hbm, y_hbm,
                 xb, xf, w, lab, mask, feat, totals, in_sem, halo_sem, out_sem, a_ref, inv_ref, w_ref, c_ref, y_ref,
                 z_ref, z_sem, out_ref, *boxes):
    rows, cin = x_hbm.shape[1], x_hbm.shape[2]
    taps, width = w_hbm.shape[0], w_hbm.shape[2]
    half = taps // 2
    chunks = cin // TILE
    size = sizes[0]
    me = lax.axis_index("frame")
    up, down = me + 1, me - 1
    has_up, has_down = me < size - 1, me > 0
    plans = [groups_of(sizes, 4)] * 3 + [groups_of(sizes, 2)]
    barrier, signals = greet(plans, size)
    load_x = pltpu.make_async_copy(x_hbm.at[0], xb.at[pl.ds(HALO, rows)], in_sem.at[0])
    load_x.start()
    load_w = pltpu.make_async_copy(w_hbm, w, in_sem.at[1])
    load_w.start()
    load_l = pltpu.make_async_copy(lab_hbm.at[0], lab, in_sem.at[2])
    load_l.start()
    for i in range(rows // TILE):
        for side in range(2):
            line = span_ref[side, 0:1, i * TILE:(i + 1) * TILE].astype(jnp.float32)
            mask[side, i * TILE:(i + 1) * TILE, :] = jnp.broadcast_to(line, (TILE, TILE)).T
    load_x.wait()

    def widen(lo, count):
        for c in range(chunks):
            xf[c, lo:lo + count, :] = xb[lo:lo + count, c * TILE:(c + 1) * TILE].astype(jnp.float32)
    widen(HALO, rows)
    load_w.wait()
    totals[...] = jnp.zeros_like(totals)

    def taps_at(at, count):
        pieces = []
        for k in range(taps):
            off = k - half
            base = HALO + at
            if off == 0:
                pieces.append(xb[base:base + count, :])
                continue
            keep = mask[0 if off < 0 else 1, at:at + count, :] >= abs(off)
            for c in range(chunks):
                v = xf[c, base + off:base + off + count, :]
                pieces.append(jnp.where(keep, v, 0.0).astype(jnp.bfloat16))
        return jnp.concatenate(pieces, axis=1)

    def block(parts):
        stacked = [taps_at(at, count) for at, count in parts]
        stacked = stacked[0] if len(stacked) == 1 else jnp.concatenate(stacked, axis=0)
        pre = jnp.dot(stacked, w[...].reshape(taps * cin, width), preferred_element_type=jnp.float32) + bias_ref[...]
        out = (0.5 * pre * (1.0 + lax.erf(pre * math.sqrt(0.5)))).astype(jnp.bfloat16)
        done = 0
        for at, count in parts:
            feat[at:at + count, :] = out[done:done + count]
            done += count
        totals[...] += jnp.sum(out.astype(jnp.float32).reshape(-1, 8, width), axis=0)

    cuts = list(range(HALO, rows - HALO, STEP)) + [rows - HALO]
    blocks = list(zip(cuts[:-1], cuts[1:]))
    block([(blocks[0][0], blocks[0][1] - blocks[0][0])])
    pl.semaphore_wait(barrier, signals)
    send_up = pltpu.make_async_remote_copy(
        src_ref=x_hbm.at[0, pl.ds(rows - HALO, HALO)], dst_ref=xb.at[pl.ds(0, HALO)],
        send_sem=halo_sem.at[0], recv_sem=halo_sem.at[1], device_id={"frame": up}, device_id_type=pl.DeviceIdType.MESH)
    send_down = pltpu.make_async_remote_copy(
        src_ref=x_hbm.at[0, pl.ds(0, HALO)], dst_ref=xb.at[pl.ds(rows + HALO, HALO)],
        send_sem=halo_sem.at[2], recv_sem=halo_sem.at[3], device_id={"frame": down}, device_id_type=pl.DeviceIdType.MESH)

    @pl.when(has_up)
    def _():
        send_up.start()

    @pl.when(has_down)
    def _():
        send_down.start()

    @pl.when(jnp.logical_not(has_down))
    def _():
        xb[:HALO, :] = jnp.zeros((HALO, cin), jnp.bfloat16)

    @pl.when(jnp.logical_not(has_up))
    def _():
        xb[rows + HALO:, :] = jnp.zeros((HALO, cin), jnp.bfloat16)

    for lo, hi in blocks[1:]:
        block([(lo, hi - lo)])

    @pl.when(has_up)
    def _():
        send_up.wait_send()
        send_down.wait_recv()

    @pl.when(has_down)
    def _():
        send_down.wait_send()
        send_up.wait_recv()

    widen(0, HALO)
    widen(rows + HALO, HALO)
    block([(0, HALO), (rows - HALO, HALO)])
    save = pltpu.make_async_copy(feat, feat_hbm.at[0], in_sem.at[3])
    save.start()
    n, m = width // TILE, lab.shape[1] // TILE
    units = TILE // 8

    def tdot(p, q):
        return lax.dot_general(p, q, (((0,), (0,)), ((), ())), preferred_element_type=jnp.float32)

    def put(ref, slot, tile):
        ref[slot * units:(slot + 1) * units] = tile.reshape(units, 8, TILE)

    streams = [
        Stream(plan, 2 * (i == len(plans) - 1), boxes[i], boxes[len(plans) + i], *boxes[2 * len(plans) + 3 * i:2 * len(plans) + 3 * i + 3])
        for i, plan in enumerate(plans)
    ]
    load_l.wait()
    ft = jnp.sum(totals[...], axis=0, keepdims=True)
    lt = jnp.sum(lab[...], axis=0, keepdims=True).astype(jnp.float32)
    hold = TILE // 2
    sums = [v[:, c:c + hold] for v in (ft, lt) for c in range(0, v.shape[1], hold)]
    corner = jnp.concatenate(sums + [jnp.zeros((hold - len(sums), hold), jnp.float32)], axis=0)
    for stream, some in zip(streams, wanted(n)):
        src = stream.src
        at = 0
        while at < len(some):
            i, j = some[at]
            run = 1
            while at + run < len(some) and some[at + run] == (i, j + run):
                run += 1
            line = tdot(feat[:, i * TILE:(i + 1) * TILE], feat[:, j * TILE:(j + run) * TILE])
            for r in range(run):
                tile = line[:, r * TILE:(r + 1) * TILE]
                if (i, j + r) == (0, 0):
                    tile = jnp.concatenate([tile[:hold], jnp.concatenate([corner, tile[hold:, hold:]], axis=1)], axis=0)
                put(src, at + r, tile)
            at += run
        if src.shape[0] > len(some) * units:
            src[len(some) * units:] = jnp.zeros((src.shape[0] - len(some) * units, 8, TILE), jnp.float32)
        stream.start()
    x_src = streams[-1].src
    left = lax.broadcasted_iota(jnp.int32, (width // 2, TILE), 1) < TILE // 2
    for j in range(m):
        flags = lab[:, j * TILE:(j + 1) * TILE].astype(jnp.float32).astype(jnp.bfloat16)
        line = tdot(feat[...], flags)
        top, low = line[:width // 2], swap_halves(line[width // 2:])
        for q, v in ((2 * j, jnp.where(left, top, low)), (2 * j + 1, jnp.where(left, low, top))):
            x_src[q * width // 16:(q + 1) * width // 16] = v.reshape(width // 16, 8, TILE)
    streams[-1].start()
    gram0, gram1, gram2, cross_sums = streams

    def step(*some):
        for stream in some:
            if not stream.done():
                stream.finish()
                if not stream.done():
                    stream.start()

    def drain(stream):
        while not stream.done():
            step(stream)

    spread_bits = [bit_values(group) for group in plans[-1][:2]]
    ranks = [rank_of(bits) for bits in spread_bits]
    block = (ranks[0] << len(spread_bits[1])) + ranks[1]
    odd = lax.rem(block, 2)
    polls = {(0, 2): [gram1], (0, 6): [cross_sums], (1, 5): [gram2], (1, 6): [cross_sums]}

    def invert(k):
        invert_block(a_ref, inv_ref, k, lambda g: step(*polls.get((k, g), [])))

    def centre_tiles(which):
        for slot, (i, j) in enumerate(wanted(n)[which]):
            tile = tile_at(streams[which].out, slot)
            centre.gram(a_ref, i, j, centre.mirror(tile) if (i, j) == (0, 0) else tile)

    step(gram0, gram1, gram2)
    step(gram0, gram1, cross_sums, gram2)
    drain(gram0)
    centre = Centre(float(rows * sizes[0] * sizes[1]), n, m, tile_at(gram0.out, 0))
    centre_tiles(0)
    invert(0)
    scale_row(a_ref, inv_ref, w_ref, 0, 1, 2)
    drain(gram1)
    centre_tiles(1)
    update(a_ref, w_ref, 0, 1, 1, 2)
    invert(1)
    drain(gram2)
    centre_tiles(2)
    scale_row(a_ref, inv_ref, w_ref, 0, 2, n)
    for i in range(1, n):
        update(a_ref, w_ref, 0, i, max(i, 2), n)
    for k in range(1, n):
        if k > 1:
            invert(k)
        if k < n - 1:
            scale_row(a_ref, inv_ref, w_ref, k, k + 1, n)
            for i in range(k + 1, n):
                update(a_ref, w_ref, k, i, i, n)
        if k == n - 2:
            drain(cross_sums)
            packed = cross_sums.out[pl.ds(block * (width // 16), width // 16)].reshape(width // 2, TILE)
            centre.cross(c_ref, block, odd, packed)
            for i in range(n - 1):
                forward(w_ref, c_ref, i)
    share = width // 4
    total = 2 * m
    near = left[:share]
    sent = [[], []]

    def pass_on(part, phase):
        group, bits = plans[-1][1 - phase], spread_bits[1 - phase]
        first = part * total + (ranks[0] * (total // 2) if phase else block)
        span = pl.ds(pl.multiple_of(first * share, share), (total // 2 if phase else 1) * share)
        for other in range(1, 1 << len(group)):
            sem = len(sent[0]) + len(sent[1])
            copy = pltpu.make_async_remote_copy(
                src_ref=z_ref.at[span], dst_ref=z_ref.at[span],
                send_sem=z_sem.at[0, sem], recv_sem=z_sem.at[1, sem],
                device_id=peer_of(group, bits, other), device_id_type=pl.DeviceIdType.MESH,
            )
            copy.start()
            sent[part].append(copy)

    def ready(k):
        for part in range(2):
            if k == part * n // 4:
                lo = part * share
                packed = jnp.where(near, y_ref[lo:lo + share, :], swap_halves(y_ref[2 * share + lo:3 * share + lo, :]))
                packed = jnp.where(odd == 1, swap_halves(packed), packed)
                at = (part * total + block) * share
                z_ref[pl.ds(pl.multiple_of(at, share), share), :] = packed.astype(jnp.bfloat16)
                pass_on(part, 0)

    backward(inv_ref, w_ref, c_ref, y_ref, ready)
    for part in (1, 0):
        for copy in sent[part]:
            copy.wait()
        pass_on(part, 1)
    for part in (1, 0):
        sent[part][-1].wait()
        for j in range(m):
            at = (part * total + 2 * j) * share
            even, uneven = [z_ref[at + q * share:at + (q + 1) * share, :].astype(jnp.float32) for q in range(2)]
            lo, cols = part * share, slice(j * TILE, (j + 1) * TILE)
            out_ref[lo:lo + share, cols] = jnp.where(near, even, uneven).astype(jnp.bfloat16)
            out_ref[2 * share + lo:3 * share + lo, cols] = swap_halves(jnp.where(near, uneven, even)).astype(jnp.bfloat16)
    leave = pltpu.make_async_copy(out_ref, y_hbm, out_sem.at[0])
    leave.start()
    leave.wait()
    save.wait()


def front(inputs, conv_weight, conv_bias, labels, rec_span):
    sizes = (lax.axis_size("frame"), lax.axis_size("rec"))
    devices = sizes[0] * sizes[1]
    rows, cin = inputs.shape[1:]
    taps, _, width = conv_weight.shape
    wide = labels.shape[2]
    n, m = width // TILE, wide // TILE
    tiles = [len(some) for some in wanted(n)] + [n * m]
    units = [-(-t * (TILE // 8) // devices) * devices for t in tiles]
    vm = pl.BlockSpec(memory_space=pltpu.VMEM)
    hbm = pl.BlockSpec(memory_space=pltpu.HBM)
    plans = [groups_of(sizes, 4)] * 3 + [groups_of(sizes, 2)]
    boxes = [v for plan, u in zip(plans, units) for v in stream_scratch(plan, u)]
    return pl.pallas_call(
        lambda *r: front_kernel(sizes, *r),
        out_shape=[jax.ShapeDtypeStruct((1, rows, width), jnp.bfloat16)]
        + [jax.ShapeDtypeStruct((width, wide), jnp.bfloat16)],
        in_specs=[hbm, hbm, vm, hbm, vm],
        out_specs=[hbm, hbm],
        scratch_shapes=[
            pltpu.VMEM((rows + 2 * HALO, cin), jnp.bfloat16),
            pltpu.VMEM((cin // TILE, rows + 2 * HALO, TILE), jnp.float32),
            pltpu.VMEM(conv_weight.shape, jnp.bfloat16),
            pltpu.VMEM((rows, wide), jnp.int32),
            pltpu.VMEM((2, rows, TILE), jnp.float32),
            pltpu.VMEM((rows, width), jnp.bfloat16),
            pltpu.VMEM((8, width), jnp.float32),
            pltpu.SemaphoreType.DMA((4,)),
            pltpu.SemaphoreType.DMA((4,)),
            pltpu.SemaphoreType.DMA((n,)),
            pltpu.VMEM((width, width), jnp.float32),
            pltpu.VMEM((width, TILE), jnp.float32),
            pltpu.VMEM((width, width), jnp.float32),
            pltpu.VMEM((width, TILE), jnp.float32),
            pltpu.VMEM((width, TILE), jnp.float32),
            pltpu.VMEM((wide * width // TILE, TILE), jnp.bfloat16),
            pltpu.SemaphoreType.DMA((2, copies_of(plans[-1][:2]))),
            pltpu.VMEM((width, wide), jnp.bfloat16),
        ] + [pltpu.VMEM((u, 8, TILE), jnp.float32) for u in units * 2] + boxes,
        compiler_params=pltpu.CompilerParams(collective_id=0, has_side_effects=True, vmem_limit_bytes=60 << 20),
    )(inputs, conv_weight, conv_bias.reshape(1, width), labels, rec_span)


def leave_kernel(feat_in, y_in, feat_out, y_out, feat, held, wide, sems):
    count = sems.shape[1] // 2
    fetch, store = [], []
    rows, lines = y_in.shape[0] // count, feat_in.shape[1] // count
    for i in range(count):
        p = pl.ds(i * rows, rows)
        fetch.append(pltpu.make_async_copy(y_in.at[p], held.at[p], sems.at[0, i]))
        store.append(pltpu.make_async_copy(wide.at[p], y_out.at[p], sems.at[1, i]))
    for i in range(count):
        p = pl.ds(i * lines, lines)
        fetch.append(pltpu.make_async_copy(feat_in.at[0, p], feat.at[p], sems.at[0, count + i]))
        store.append(pltpu.make_async_copy(feat.at[p], feat_out.at[0, p], sems.at[1, count + i]))
    for copy in fetch:
        copy.start()
    for i in range(2 * count):
        fetch[i].wait()
        if i < count:
            wide[i * rows:(i + 1) * rows, :] = held[i * rows:(i + 1) * rows, :].astype(jnp.float32)
        store[i].start()
    for copy in store:
        copy.wait()


def leave(features, y):
    hbm = pl.BlockSpec(memory_space=pltpu.HBM)
    return pl.pallas_call(
        leave_kernel,
        out_shape=[jax.ShapeDtypeStruct(features.shape, features.dtype), jax.ShapeDtypeStruct(y.shape, jnp.float32)],
        in_specs=[hbm, hbm],
        out_specs=[hbm, hbm],
        scratch_shapes=[
            pltpu.VMEM(features.shape[1:], features.dtype),
            pltpu.VMEM(y.shape, y.dtype),
            pltpu.VMEM(y.shape, jnp.float32),
            pltpu.SemaphoreType.DMA((2, 4)),
        ],
        compiler_params=pltpu.CompilerParams(vmem_limit_bytes=60 << 20),
    )(features, y)


def per_device(inputs, conv_weight, conv_bias, labels, rec_span):
    features, probe_weights = front(inputs, conv_weight, conv_bias, labels, rec_span)
    return tuple(leave(features, probe_weights))


def solution(mesh):
    in_specs = (P("rec", "frame", None), P(), P(), P("rec", "frame", None), P(None, "rec", "frame"))
    out_specs = (P("rec", "frame", None), P())
    return jax.shard_map(
        per_device, mesh=mesh, in_specs=in_specs, out_specs=out_specs, check_vma=False
    )
```

```python
import math
import jax
import jax.numpy as jnp
from jax import lax
from jax.experimental import pallas as pl
from jax.experimental.pallas import tpu as pltpu
from jax.sharding import PartitionSpec as P

RIDGE = 0.1
TILE = 128
HI = lax.Precision.HIGHEST
GROUP = 16
HALO = 16
STEP = 256

def mm(a, b):
    return jnp.dot(a, b, precision=HI, preferred_element_type=jnp.float32)

def mtm(a, b):
    return lax.dot_general(a, b, (((0,), (0,)), ((), ())), precision=HI, preferred_element_type=jnp.float32)

def spread(row, width):
    return jnp.broadcast_to(row, (8, width))

def tree(terms):
    while len(terms) > 1:
        terms = [terms[i] + terms[i + 1] if i + 1 < len(terms) else terms[i] for i in range(0, len(terms), 2)]
    return terms[0]

def invert_tile(slabs, between):
    count = len(slabs)
    width = 8 * count
    lane = lax.broadcasted_iota(jnp.int32, (8, width), 1)
    sub = lax.broadcasted_iota(jnp.int32, (8, width), 0)
    homes = GROUP // 8
    zero = jnp.zeros((8, width), jnp.float32)
    for j in range(0, width, GROUP):
        first = j // 8
        in_group = (lane >= j) & (lane < j + GROUP)
        near = list(range(first, min(count, first + 2 * homes)))
        cols = {i: [jnp.broadcast_to(slabs[i][:, j + b:j + b + 1], (8, width)) for b in range(GROUP)] for i in near}
        hc = [list(cols[first + t]) for t in range(homes)]
        u = [jnp.where(in_group, jnp.where(lane - sub == j + 8 * t, 1.0, 0.0), slabs[first + t]) for t in range(homes)]
        scale = [jnp.ones((8, width), jnp.float32)] * homes
        for p in range(GROUP):
            h, s = p // 8, p % 8
            r = 1.0 / spread(hc[h][p][s:s + 1], width)
            m = [jnp.where(sub == s, 0.0, hc[t][p]) if t == h else hc[t][p] for t in range(homes)]
            for b in range(p + 1, GROUP):
                f = spread(hc[h][b][s:s + 1], width) * r
                for t in range(homes):
                    hc[t][b] = hc[t][b] - m[t] * f
            row = spread(u[h][s:s + 1], width) * r
            for t in range(homes):
                u[t] = u[t] - m[t] * row
            scale[h] = jnp.where(sub == s, r, scale[h])
        u = [u[t] * scale[t] for t in range(homes)]
        fresh = list(slabs)
        for t in range(homes):
            fresh[first + t] = u[t]
        nxt = near[homes:]
        if nxt:
            rows = [spread(u[b // 8][b % 8:b % 8 + 1], width) for b in range(GROUP)]
            for i in nxt:
                fresh[i] = jnp.where(in_group, 0.0, slabs[i]) - tree([cols[i][b] * rows[b] for b in range(GROUP)])
        left = jnp.concatenate(slabs, axis=0)
        right = jnp.concatenate([u[i - first] if first <= i < first + homes else zero for i in range(count)], axis=0)
        prod = mm(left, right)
        for i in range(count):
            if i not in near:
                fresh[i] = jnp.where(in_group, 0.0, slabs[i]) - prod[8 * i:8 * i + 8]
        slabs = fresh
        between(j // GROUP)
    return slabs

def invert_block(a_ref, inv_ref, k, between):
    lo, hi = k * TILE, (k + 1) * TILE
    slabs = invert_tile([a_ref[lo + 8 * i:lo + 8 * i + 8, lo:hi] for i in range(TILE // 8)], between)
    for i, s in enumerate(slabs):
        inv_ref[lo + 8 * i:lo + 8 * i + 8, :] = s


def scale_row(a_ref, inv_ref, w_ref, k, first, last):
    lo, hi = k * TILE, (k + 1) * TILE
    s = slice(first * TILE, last * TILE)
    w_ref[lo:hi, s] = mm(inv_ref[lo:hi, :], a_ref[lo:hi, s])


def update(a_ref, w_ref, k, i, first, last):
    lo, hi = k * TILE, (k + 1) * TILE
    s = slice(first * TILE, last * TILE)
    rows = slice(i * TILE, (i + 1) * TILE)
    a_ref[rows, s] -= mtm(a_ref[lo:hi, rows], w_ref[lo:hi, s])


def forward(w_ref, c_ref, k):
    lo, hi = k * TILE, (k + 1) * TILE
    c_ref[hi:, :] -= mtm(w_ref[lo:hi, hi:], c_ref[lo:hi, :])


def backward(inv_ref, w_ref, c_ref, y_ref, ready):
    n = y_ref.shape[0] // TILE
    for k in reversed(range(n)):
        lo, hi = k * TILE, (k + 1) * TILE
        y = mm(inv_ref[lo:hi, :], c_ref[lo:hi, :])
        if k < n - 1:
            y = y - mm(w_ref[lo:hi, hi:], y_ref[hi:, :])
        y_ref[lo:hi, :] = y
        ready(k)


def swap_halves(v):
    return pltpu.roll(v, TILE // 2, 1)


def bits_of(axis, size):
    return [(axis, 1 << i) for i in range(size.bit_length() - 1)]


def pairs(n):
    return [(i, j) for i in range(n) for j in range(i, n)]


def wanted(n):
    first = [(0, 0), (0, 1), (1, 1), (0, 2)]
    return [first[:2], first[2:], [p for p in pairs(n) if p not in first]]


def groups_of(sizes, most):
    frame, rec = bits_of("frame", sizes[0]), bits_of("rec", sizes[1])
    rest = rec[1:2] + frame[:1] + frame[1:] + rec[2:]
    return [rec[:1]] + [rest[i:i + most] for i in range(0, len(rest), most)]


def bit_values(group):
    return [lax.rem(lax.axis_index(axis) // step, 2) for axis, step in group]


def peer_of(group, bits, mask):
    place = {}
    for i, (axis, step) in enumerate(group):
        if mask >> i & 1:
            place[axis] = place.get(axis, lax.axis_index(axis)) + (1 - 2 * bits[i]) * step
    return place


def rank_of(bits, mask=0):
    return sum((1 - v if mask >> i & 1 else v) * (1 << i) for i, v in enumerate(bits))


def inbox_units(groups, units):
    total = 0
    for group in groups:
        chunk = units >> len(group)
        total += units - chunk
        units = chunk
    return total


def copies_of(groups):
    return 2 * sum((1 << len(g)) - 1 for g in groups)


class Stream:
    def __init__(self, groups, split, src, out, acc, inbox, sems):
        self.phases = 2 * len(groups) - split
        self.groups, self.src, self.out, self.acc, self.inbox, self.sems = groups, src, out, acc, inbox, sems
        self.length, self.lo, self.at = src.shape[0], 0, 0
        self.held, self.used, self.kept, self.sem = (src, 0), 0, 0, 0
        self.copies = []

    def done(self):
        return self.at == self.phases

    def start(self):
        count = len(self.groups)
        self.down = self.at < count
        self.group = self.groups[self.at if self.down else 2 * count - 1 - self.at]
        self.bits = bit_values(self.group)
        self.copies = []
        self.chunk = self.length >> len(self.group)
        for mask in range(1, 1 << len(self.group)):
            if self.down:
                ref, base = self.held
                src = ref.at[pl.ds(base + rank_of(self.bits, mask) * self.chunk, self.chunk)]
                dst = self.inbox.at[pl.ds(self.used + (mask - 1) * self.chunk, self.chunk)]
            else:
                src = dst = self.out.at[pl.ds(self.lo, self.length)]
            copy = pltpu.make_async_remote_copy(
                src_ref=src, dst_ref=dst,
                send_sem=self.sems.at[0, self.sem], recv_sem=self.sems.at[1, self.sem],
                device_id=peer_of(self.group, self.bits, mask), device_id_type=pl.DeviceIdType.MESH,
            )
            copy.start()
            self.copies.append(copy)
            self.sem += 1

    def finish(self):
        for copy in self.copies:
            copy.wait()
        rank = rank_of(self.bits)
        if self.down:
            ref, base = self.held
            total = ref[pl.ds(base + rank * self.chunk, self.chunk)]
            for i in range((1 << len(self.group)) - 1):
                total = total + self.inbox[self.used + i * self.chunk:self.used + (i + 1) * self.chunk]
            self.used += self.length - self.chunk
            self.lo, self.length = self.lo + rank * self.chunk, self.chunk
            if self.at < len(self.groups) - 1:
                self.acc[self.kept:self.kept + self.chunk] = total
                self.held = (self.acc, self.kept)
                self.kept += self.chunk
            else:
                self.out[pl.ds(self.lo, self.chunk)] = total
        else:
            self.lo = self.lo - rank * self.length
            self.length = self.length << len(self.group)
        self.at += 1


def stream_scratch(groups, units):
    held = sum(units >> sum(len(g) for g in groups[:i + 1]) for i in range(len(groups) - 1))
    return [
        pltpu.VMEM((max(held, 1), 8, TILE), jnp.float32),
        pltpu.VMEM((inbox_units(groups, units), 8, TILE), jnp.float32),
        pltpu.SemaphoreType.DMA((2, copies_of(groups))),
    ]


def greet(plans, size):
    barrier = pltpu.get_barrier_semaphore()
    met = {}
    for groups in plans:
        for group in groups:
            for mask in range(1, 1 << len(group)):
                met[tuple(sorted(bit for i, bit in enumerate(group) if mask >> i & 1))] = (group, mask)
    for group, mask in met.values():
        pl.semaphore_signal(barrier, inc=1, device_id=peer_of(group, bit_values(group), mask), device_id_type=pl.DeviceIdType.MESH)
    me = lax.axis_index("frame")
    for there, peer in ((me < size - 1, me + 1), (me > 0, me - 1)):
        @pl.when(there)
        def _():
            pl.semaphore_signal(barrier, inc=1, device_id={"frame": peer}, device_id_type=pl.DeviceIdType.MESH)
    return barrier, len(met) + 2 - jnp.where(me == 0, 1, 0) - jnp.where(me == size - 1, 1, 0)


def tile_at(ref, slot):
    units = TILE // 8
    return ref[slot * units:(slot + 1) * units].reshape(TILE, TILE)


def column(totals, i):
    return jnp.broadcast_to(totals[i:i + 1], (TILE, TILE)).T


class Centre:
    def __init__(self, frames, n, m, head):
        hold = TILE // 2
        sums = head[hold:, :hold]
        self.frames, self.n = frames, n
        self.totals = jnp.concatenate(
            [jnp.concatenate([sums[2 * i:2 * i + 1], sums[2 * i + 1:2 * i + 2]], axis=1) for i in range(n + m)], axis=0)
        self.cols = [column(self.totals, i) for i in range(n)]
        self.down = lax.broadcasted_iota(jnp.int32, (TILE, TILE), 0)
        self.across = lax.broadcasted_iota(jnp.int32, (TILE, TILE), 1)

    def mirror(self, tile):
        return jnp.where(self.down <= self.across, tile, tile.T)

    def gram(self, a_ref, i, j, tile):
        v = (tile - self.cols[i] * self.totals[j:j + 1] / self.frames) / self.frames
        if i == j:
            v = v + jnp.where(self.down == self.across, RIDGE, 0.0)
        a_ref[i * TILE:(i + 1) * TILE, j * TILE:(j + 1) * TILE] = v

    def cross(self, c_ref, block, own, packed):
        labels = jnp.zeros((1, TILE), jnp.float32)
        for q in range(2 * (self.totals.shape[0] - self.n)):
            line = self.totals[self.n + q // 2:self.n + q // 2 + 1]
            labels = jnp.where(block == q, swap_halves(line) if q % 2 else line, labels)
        packed = jnp.where(own == 1, swap_halves(packed), packed)
        rows = packed.shape[0]
        for at, part in ((0, packed), (rows, swap_halves(packed))):
            for i in range(rows // TILE):
                lo = at + i * TILE
                v = part[i * TILE:(i + 1) * TILE] - self.cols[lo // TILE] * labels / self.frames
                c_ref[lo:lo + TILE, :] = v / math.sqrt(self.frames)


def front_kernel(sizes, x_hbm, w_hbm, bias_ref, lab_hbm, span_ref, feat_hbm, y_hbm,
                 xb, xf, w, lab, mask, feat, totals, in_sem, halo_sem, out_sem, a_ref, inv_ref, w_ref, c_ref, y_ref,
                 z_ref, z_sem, out_ref, *boxes):
    rows, cin = x_hbm.shape[1], x_hbm.shape[2]
    taps, width = w_hbm.shape[0], w_hbm.shape[2]
    half = taps // 2
    chunks = cin // TILE
    size = sizes[0]
    me = lax.axis_index("frame")
    up, down = me + 1, me - 1
    has_up, has_down = me < size - 1, me > 0
    plans = [groups_of(sizes, 4)] * 3 + [groups_of(sizes, 2)]
    barrier, signals = greet(plans, size)
    load_x = pltpu.make_async_copy(x_hbm.at[0], xb.at[pl.ds(HALO, rows)], in_sem.at[0])
    load_x.start()
    load_w = pltpu.make_async_copy(w_hbm, w, in_sem.at[1])
    load_w.start()
    load_l = pltpu.make_async_copy(lab_hbm.at[0], lab, in_sem.at[2])
    load_l.start()
    for i in range(rows // TILE):
        for side in range(2):
            line = span_ref[side, 0:1, i * TILE:(i + 1) * TILE].astype(jnp.float32)
            mask[side, i * TILE:(i + 1) * TILE, :] = jnp.broadcast_to(line, (TILE, TILE)).T
    load_x.wait()

    def widen(lo, count):
        for c in range(chunks):
            xf[c, lo:lo + count, :] = xb[lo:lo + count, c * TILE:(c + 1) * TILE].astype(jnp.float32)
    widen(HALO, rows)
    load_w.wait()
    totals[...] = jnp.zeros_like(totals)

    def taps_at(at, count):
        pieces = []
        for k in range(taps):
            off = k - half
            base = HALO + at
            if off == 0:
                pieces.append(xb[base:base + count, :])
                continue
            keep = mask[0 if off < 0 else 1, at:at + count, :] >= abs(off)
            for c in range(chunks):
                v = xf[c, base + off:base + off + count, :]
                pieces.append(jnp.where(keep, v, 0.0).astype(jnp.bfloat16))
        return jnp.concatenate(pieces, axis=1)

    def block(parts):
        stacked = [taps_at(at, count) for at, count in parts]
        stacked = stacked[0] if len(stacked) == 1 else jnp.concatenate(stacked, axis=0)
        pre = jnp.dot(stacked, w[...].reshape(taps * cin, width), preferred_element_type=jnp.float32) + bias_ref[...]
        out = (0.5 * pre * (1.0 + lax.erf(pre * math.sqrt(0.5)))).astype(jnp.bfloat16)
        done = 0
        for at, count in parts:
            feat[at:at + count, :] = out[done:done + count]
            done += count
        totals[...] += jnp.sum(out.astype(jnp.float32).reshape(-1, 8, width), axis=0)

    cuts = list(range(HALO, rows - HALO, STEP)) + [rows - HALO]
    blocks = list(zip(cuts[:-1], cuts[1:]))
    block([(blocks[0][0], blocks[0][1] - blocks[0][0])])
    pl.semaphore_wait(barrier, signals)
    send_up = pltpu.make_async_remote_copy(
        src_ref=x_hbm.at[0, pl.ds(rows - HALO, HALO)], dst_ref=xb.at[pl.ds(0, HALO)],
        send_sem=halo_sem.at[0], recv_sem=halo_sem.at[1], device_id={"frame": up}, device_id_type=pl.DeviceIdType.MESH)
    send_down = pltpu.make_async_remote_copy(
        src_ref=x_hbm.at[0, pl.ds(0, HALO)], dst_ref=xb.at[pl.ds(rows + HALO, HALO)],
        send_sem=halo_sem.at[2], recv_sem=halo_sem.at[3], device_id={"frame": down}, device_id_type=pl.DeviceIdType.MESH)

    @pl.when(has_up)
    def _():
        send_up.start()

    @pl.when(has_down)
    def _():
        send_down.start()

    @pl.when(jnp.logical_not(has_down))
    def _():
        xb[:HALO, :] = jnp.zeros((HALO, cin), jnp.bfloat16)

    @pl.when(jnp.logical_not(has_up))
    def _():
        xb[rows + HALO:, :] = jnp.zeros((HALO, cin), jnp.bfloat16)

    for lo, hi in blocks[1:]:
        block([(lo, hi - lo)])
    load_l.wait()
    lt = jnp.sum(lab[...], axis=0, keepdims=True).astype(jnp.float32)

    @pl.when(has_up)
    def _():
        send_up.wait_send()
        send_down.wait_recv()

    @pl.when(has_down)
    def _():
        send_down.wait_send()
        send_up.wait_recv()

    widen(0, HALO)
    widen(rows + HALO, HALO)
    block([(0, HALO), (rows - HALO, HALO)])
    save = pltpu.make_async_copy(feat, feat_hbm.at[0], in_sem.at[3])
    save.start()
    n, m = width // TILE, lab.shape[1] // TILE
    units = TILE // 8

    def tdot(p, q):
        return lax.dot_general(p, q, (((0,), (0,)), ((), ())), preferred_element_type=jnp.float32)

    def put(ref, slot, tile):
        ref[slot * units:(slot + 1) * units] = tile.reshape(units, 8, TILE)

    streams = [
        Stream(plan, 2 * (i == len(plans) - 1), boxes[i], boxes[len(plans) + i], *boxes[2 * len(plans) + 3 * i:2 * len(plans) + 3 * i + 3])
        for i, plan in enumerate(plans)
    ]
    ft = jnp.sum(totals[...], axis=0, keepdims=True)
    hold = TILE // 2
    sums = [v[:, c:c + hold] for v in (ft, lt) for c in range(0, v.shape[1], hold)]
    corner = jnp.concatenate(sums + [jnp.zeros((hold - len(sums), hold), jnp.float32)], axis=0)
    for stream, some in zip(streams, wanted(n)):
        src = stream.src
        at = 0
        while at < len(some):
            i, j = some[at]
            run = 1
            while at + run < len(some) and some[at + run] == (i, j + run):
                run += 1
            line = tdot(feat[:, i * TILE:(i + 1) * TILE], feat[:, j * TILE:(j + run) * TILE])
            for r in range(run):
                tile = line[:, r * TILE:(r + 1) * TILE]
                if (i, j + r) == (0, 0):
                    tile = jnp.concatenate([tile[:hold], jnp.concatenate([corner, tile[hold:, hold:]], axis=1)], axis=0)
                put(src, at + r, tile)
            at += run
        if src.shape[0] > len(some) * units:
            src[len(some) * units:] = jnp.zeros((src.shape[0] - len(some) * units, 8, TILE), jnp.float32)
        stream.start()
    x_src = streams[-1].src
    left = lax.broadcasted_iota(jnp.int32, (width // 2, TILE), 1) < TILE // 2
    for j in range(m):
        flags = lab[:, j * TILE:(j + 1) * TILE].astype(jnp.float32).astype(jnp.bfloat16)
        line = tdot(feat[...], flags)
        top, low = line[:width // 2], swap_halves(line[width // 2:])
        for q, v in ((2 * j, jnp.where(left, top, low)), (2 * j + 1, jnp.where(left, low, top))):
            x_src[q * width // 16:(q + 1) * width // 16] = v.reshape(width // 16, 8, TILE)
    streams[-1].start()
    gram0, gram1, gram2, cross_sums = streams

    def step(*some):
        for stream in some:
            if not stream.done():
                stream.finish()
                if not stream.done():
                    stream.start()

    def drain(stream):
        while not stream.done():
            step(stream)

    spread_bits = [bit_values(group) for group in plans[-1][:2]]
    ranks = [rank_of(bits) for bits in spread_bits]
    block = (ranks[0] << len(spread_bits[1])) + ranks[1]
    odd = lax.rem(block, 2)
    polls = {(0, 2): [gram1], (0, 6): [cross_sums], (1, 5): [gram2], (1, 6): [cross_sums]}

    def invert(k):
        invert_block(a_ref, inv_ref, k, lambda g: step(*polls.get((k, g), [])))

    def centre_tiles(which):
        for slot, (i, j) in enumerate(wanted(n)[which]):
            tile = tile_at(streams[which].out, slot)
            centre.gram(a_ref, i, j, centre.mirror(tile) if (i, j) == (0, 0) else tile)

    step(gram0, gram1, gram2)
    step(gram0, gram1, cross_sums, gram2)
    drain(gram0)
    centre = Centre(float(rows * sizes[0] * sizes[1]), n, m, tile_at(gram0.out, 0))
    centre_tiles(0)
    invert(0)
    scale_row(a_ref, inv_ref, w_ref, 0, 1, 2)
    drain(gram1)
    centre_tiles(1)
    update(a_ref, w_ref, 0, 1, 1, 2)
    invert(1)
    drain(gram2)
    centre_tiles(2)
    scale_row(a_ref, inv_ref, w_ref, 0, 2, n)
    for i in range(1, n):
        update(a_ref, w_ref, 0, i, max(i, 2), n)
    for k in range(1, n):
        if k > 1:
            invert(k)
        if k < n - 1:
            scale_row(a_ref, inv_ref, w_ref, k, k + 1, n)
            for i in range(k + 1, n):
                update(a_ref, w_ref, k, i, i, n)
        if k == n - 2:
            drain(cross_sums)
            packed = cross_sums.out[pl.ds(block * (width // 16), width // 16)].reshape(width // 2, TILE)
            centre.cross(c_ref, block, odd, packed)
            for i in range(n - 1):
                forward(w_ref, c_ref, i)
    share = width // 4
    total = 2 * m
    near = left[:share]
    sent = [[], []]

    def pass_on(part, phase):
        group, bits = plans[-1][1 - phase], spread_bits[1 - phase]
        first = part * total + (ranks[0] * (total // 2) if phase else block)
        span = pl.ds(pl.multiple_of(first * share, share), (total // 2 if phase else 1) * share)
        for other in range(1, 1 << len(group)):
            sem = len(sent[0]) + len(sent[1])
            copy = pltpu.make_async_remote_copy(
                src_ref=z_ref.at[span], dst_ref=z_ref.at[span],
                send_sem=z_sem.at[0, sem], recv_sem=z_sem.at[1, sem],
                device_id=peer_of(group, bits, other), device_id_type=pl.DeviceIdType.MESH,
            )
            copy.start()
            sent[part].append(copy)

    def ready(k):
        for part in range(2):
            if k == part * n // 4:
                lo = part * share
                packed = jnp.where(near, y_ref[lo:lo + share, :], swap_halves(y_ref[2 * share + lo:3 * share + lo, :]))
                packed = jnp.where(odd == 1, swap_halves(packed), packed)
                at = (part * total + block) * share
                z_ref[pl.ds(pl.multiple_of(at, share), share), :] = packed.astype(jnp.bfloat16)
                pass_on(part, 0)

    backward(inv_ref, w_ref, c_ref, y_ref, ready)
    for part in (1, 0):
        for copy in sent[part]:
            copy.wait()
        pass_on(part, 1)
    leaving = []
    for part in (1, 0):
        sent[part][-1].wait()
        for j in range(m):
            at = (part * total + 2 * j) * share
            even, uneven = [z_ref[at + q * share:at + (q + 1) * share, :].astype(jnp.float32) for q in range(2)]
            lo, cols = part * share, slice(j * TILE, (j + 1) * TILE)
            out_ref[lo:lo + share, cols] = jnp.where(near, even, uneven).astype(jnp.bfloat16)
            out_ref[2 * share + lo:3 * share + lo, cols] = swap_halves(jnp.where(near, uneven, even)).astype(jnp.bfloat16)
        for side in range(2):
            span = pl.ds((2 * side + part) * share, share)
            copy = pltpu.make_async_copy(out_ref.at[span], y_hbm.at[span], out_sem.at[2 * side + part])
            copy.start()
            leaving.append(copy)
    for copy in leaving:
        copy.wait()
    save.wait()


def front(inputs, conv_weight, conv_bias, labels, rec_span):
    sizes = (lax.axis_size("frame"), lax.axis_size("rec"))
    devices = sizes[0] * sizes[1]
    rows, cin = inputs.shape[1:]
    taps, _, width = conv_weight.shape
    wide = labels.shape[2]
    n, m = width // TILE, wide // TILE
    tiles = [len(some) for some in wanted(n)] + [n * m]
    units = [-(-t * (TILE // 8) // devices) * devices for t in tiles]
    vm = pl.BlockSpec(memory_space=pltpu.VMEM)
    hbm = pl.BlockSpec(memory_space=pltpu.HBM)
    plans = [groups_of(sizes, 4)] * 3 + [groups_of(sizes, 2)]
    boxes = [v for plan, u in zip(plans, units) for v in stream_scratch(plan, u)]
    return pl.pallas_call(
        lambda *r: front_kernel(sizes, *r),
        out_shape=[jax.ShapeDtypeStruct((1, rows, width), jnp.bfloat16)]
        + [jax.ShapeDtypeStruct((width, wide), jnp.bfloat16)],
        in_specs=[hbm, hbm, vm, hbm, vm],
        out_specs=[hbm, hbm],
        scratch_shapes=[
            pltpu.VMEM((rows + 2 * HALO, cin), jnp.bfloat16),
            pltpu.VMEM((cin // TILE, rows + 2 * HALO, TILE), jnp.float32),
            pltpu.VMEM(conv_weight.shape, jnp.bfloat16),
            pltpu.VMEM((rows, wide), jnp.int32),
            pltpu.VMEM((2, rows, TILE), jnp.float32),
            pltpu.VMEM((rows, width), jnp.bfloat16),
            pltpu.VMEM((8, width), jnp.float32),
            pltpu.SemaphoreType.DMA((4,)),
            pltpu.SemaphoreType.DMA((4,)),
            pltpu.SemaphoreType.DMA((4,)),
            pltpu.VMEM((width, width), jnp.float32),
            pltpu.VMEM((width, TILE), jnp.float32),
            pltpu.VMEM((width, width), jnp.float32),
            pltpu.VMEM((width, TILE), jnp.float32),
            pltpu.VMEM((width, TILE), jnp.float32),
            pltpu.VMEM((wide * width // TILE, TILE), jnp.bfloat16),
            pltpu.SemaphoreType.DMA((2, copies_of(plans[-1][:2]))),
            pltpu.VMEM((width, wide), jnp.bfloat16),
        ] + [pltpu.VMEM((u, 8, TILE), jnp.float32) for u in units * 2] + boxes,
        compiler_params=pltpu.CompilerParams(collective_id=0, has_side_effects=True, vmem_limit_bytes=60 << 20),
    )(inputs, conv_weight, conv_bias.reshape(1, width), labels, rec_span)


def leave_kernel(feat_in, y_in, feat_out, y_out, feat, held, wide, sems):
    count = sems.shape[1] // 2
    fetch, store = [], []
    rows, lines = y_in.shape[0] // count, feat_in.shape[1] // count
    for i in range(count):
        p = pl.ds(i * rows, rows)
        fetch.append(pltpu.make_async_copy(y_in.at[p], held.at[p], sems.at[0, i]))
        store.append(pltpu.make_async_copy(wide.at[p], y_out.at[p], sems.at[1, i]))
    for i in range(count):
        p = pl.ds(i * lines, lines)
        fetch.append(pltpu.make_async_copy(feat_in.at[0, p], feat.at[p], sems.at[0, count + i]))
        store.append(pltpu.make_async_copy(feat.at[p], feat_out.at[0, p], sems.at[1, count + i]))
    for copy in fetch:
        copy.start()
    for i in range(2 * count):
        fetch[i].wait()
        if i < count:
            wide[i * rows:(i + 1) * rows, :] = held[i * rows:(i + 1) * rows, :].astype(jnp.float32)
        store[i].start()
    for copy in store:
        copy.wait()


def leave(features, y):
    hbm = pl.BlockSpec(memory_space=pltpu.HBM)
    return pl.pallas_call(
        leave_kernel,
        out_shape=[jax.ShapeDtypeStruct(features.shape, features.dtype), jax.ShapeDtypeStruct(y.shape, jnp.float32)],
        in_specs=[hbm, hbm],
        out_specs=[hbm, hbm],
        scratch_shapes=[
            pltpu.VMEM(features.shape[1:], features.dtype),
            pltpu.VMEM(y.shape, y.dtype),
            pltpu.VMEM(y.shape, jnp.float32),
            pltpu.SemaphoreType.DMA((2, 4)),
        ],
        compiler_params=pltpu.CompilerParams(vmem_limit_bytes=60 << 20),
    )(features, y)


def per_device(inputs, conv_weight, conv_bias, labels, rec_span):
    features, probe_weights = front(inputs, conv_weight, conv_bias, labels, rec_span)
    return tuple(leave(features, probe_weights))


def solution(mesh):
    in_specs = (P("rec", "frame", None), P(), P(), P("rec", "frame", None), P(None, "rec", "frame"))
    out_specs = (P("rec", "frame", None), P())
    return jax.shard_map(
        per_device, mesh=mesh, in_specs=in_specs, out_specs=out_specs, check_vma=False
    )
```
